32 devices in a mesh: groups: 2 (over y), var: 4 (over z), probe: 2 (over x), rep: 2 (over core).
Axes of the slice: x: 2, y: 2, z: 4, core: 2. Of those that a mesh axis runs over, the one named last changes fastest.
Arguments:
- block_values: bfloat16 [512, 6, 128, 128], P(('groups', 'var'), 'rep'), parts along dimension 0, may hold values from -6 to 6
- columns: int32 [512, 6], P(('groups', 'var'), 'rep'), parts along dimension 0, may hold values from 0 to 255, as said below
- probe_signs: int32 [512, 24, 128], P('groups', 'probe'), parts along dimension 0, may hold values from -1 to 1, as said below
Outputs:
- gradient: bfloat16 [512, 6, 128, 128], P(('groups', 'var'), 'rep'), parts along dimension 0
The draws below stay inside these ranges and needn't reach their ends.
There are 2 independent parts, one for each index of `groups`. The reference program is written for one: setup_inputs(seed, part) draws one part's arguments, and reference() takes and returns one part's arrays. A program takes and returns all parts, laid end to end along the dimension named above; each array names one. Nothing has to cross between parts.
Inputs may be any that keep to these rules, and one draw needn't show every extreme that they name: The 6 block columns of each block row are distinct. `probe_signs`: every entry is -1 or 1.
All inputs are finite; a program needn't handle non-finite values.
Results may differ from the reference program's by a relative error of at most 0.015.
Values may be sent and summed in bfloat16 or wider, within the bound.
No kernel may reach another device: no remote copies, remote signals or barrier semaphores. Data moves between devices by JAX's collectives and lax.ppermute only.
A program may use at most 128 MiB of HBM per device.

```python
import math
import jax
import jax.numpy as jnp
from jax import lax

BLK = 128
KS = 6
NB = 256
S = 24
N_VAR = 4
N_REP = 2


def draw_columns(key, part):
    scores = jax.random.randint(key, (NB, NB), 0, 1 << 20) * NB + jnp.arange(NB, dtype=jnp.int32)[None, :]
    picked = lax.top_k(scores, KS)[1]
    return picked.astype(jnp.int32)


def draw_probe_signs(key, part):
    return (2 * jax.random.randint(key, (NB, S, BLK), 0, 2) - 1).astype(jnp.int32)


def level_of(key, shape, cuts, low, high):
    def one(dim, shards_of):
        draws = jax.random.uniform(jax.random.fold_in(jax.random.fold_in(key, 6), dim), (shards_of,), jnp.float32, low / len(cuts), high / len(cuts))
        return jnp.repeat(jnp.exp(draws), shape[dim] // shards_of).reshape((-1,) + (1,) * (len(shape) - dim - 1))

    gain = one(*cuts[0])
    for cut in cuts[1:]:
        gain = gain * one(*cut)
    return gain


def scatter_about(stream_key, extent, width, limit, shards=(), kind=jnp.bfloat16):
    array = jax.random.normal(stream_key, extent, jnp.float32) * width
    if len(shards) > 0:
        array = level_of(stream_key, extent, shards, -0.22, 0.18) * array
    return jnp.clip(array, min=-limit, max=limit).astype(kind)


def setup_inputs(seed: int = 0, part: int = 0) -> dict:
    streams_of = jax.random.split(jax.random.key(seed), 4)
    own_keys = jax.random.split(jax.random.fold_in(streams_of[3], part), 4)
    block_values = scatter_about(own_keys[0], (NB, KS, BLK, BLK), 1.0, 6.0, ((0, 4), (1, 2)))
    columns = draw_columns(jax.random.fold_in(jax.random.fold_in(streams_of[3], part), 71), part)
    probe_signs = draw_probe_signs(jax.random.fold_in(jax.random.fold_in(streams_of[3], part), 71), part)
    return dict(block_values=block_values, columns=columns, probe_signs=probe_signs)


def reference(block_values, columns, probe_signs):
    inverse = 1.0 / math.sqrt(KS * BLK)
    values_wide = block_values.astype(jnp.float32)
    column_list = columns.reshape(-1)
    rows_group = NB // N_VAR
    slots_half = KS // N_REP

    def select(panel_now):
        return jnp.take(panel_now, column_list, axis=0).reshape(NB, KS, S, BLK)

    def forward(panel_now):
        product = jnp.einsum('rkij,rksj->rsi', values_wide, select(panel_now).astype(jnp.float32))
        return (panel_now.astype(jnp.float32) + inverse * product).astype(jnp.bfloat16)

    def transpose(panel_now):
        summed = jnp.zeros((NB, S, BLK), jnp.float32)
        for group_index in range(N_VAR):
            for half_index in range(N_REP):
                row_lo = group_index * rows_group
                slot_lo = half_index * slots_half
                vals = values_wide[row_lo:row_lo + rows_group, slot_lo:slot_lo + slots_half]
                weighted = jnp.einsum('rkij,rsi->rksj', vals, panel_now[row_lo:row_lo + rows_group].astype(jnp.float32))
                weighted = weighted.reshape(-1, S, BLK)
                targets = columns[row_lo:row_lo + rows_group, slot_lo:slot_lo + slots_half].reshape(-1)
                partial_value = jax.ops.segment_sum(weighted, targets, num_segments=NB)
                rounded = lax.optimization_barrier(partial_value.astype(jnp.bfloat16))
                summed = summed + rounded.astype(jnp.float32)
        return (panel_now.astype(jnp.float32) + inverse * summed).astype(jnp.bfloat16)
    start_panel = probe_signs.astype(jnp.bfloat16)
    forward_panels = [start_panel]
    back_panels = [start_panel]
    for step_index in range(3):
        forward_panels.append(forward(forward_panels[step_index]))
        back_panels.append(transpose(back_panels[step_index]))
    estimate = jnp.zeros((NB, KS, BLK, BLK), jnp.float32)
    for step_index in range(4):
        right_blocks = select(forward_panels[3 - step_index]).astype(jnp.float32)
        estimate = estimate + jnp.einsum('rsi,rksj->rkij', back_panels[step_index].astype(jnp.float32), right_blocks)
    return (estimate / S).astype(jnp.bfloat16)
```

```python
import functools
import math

import jax
import jax.numpy as jnp
from jax import lax
from jax.experimental import pallas as pl
from jax.experimental.pallas import tpu as pltpu
from jax.sharding import PartitionSpec as P

KS = 6
PAD = 16
VMEM_LIMIT = 40 * 1024 * 1024


def whole():
    return pl.BlockSpec(memory_space=pltpu.VMEM)


def params():
    return pltpu.CompilerParams(
        dimension_semantics=("arbitrary",), vmem_limit_bytes=VMEM_LIMIT
    )


def split_pair(pair, count):
    wide = pair.astype(jnp.float32)
    keep = lax.broadcasted_iota(jnp.int32, (PAD, wide.shape[1]), 0) < count
    first = jnp.where(keep, wide[:PAD], 0.0)
    second = jnp.where(keep, pltpu.roll(wide, count, 0)[:PAD], 0.0)
    return first, second


def join_pair(first, second, count):
    tail = jnp.zeros((2 * count - PAD, first.shape[1]), jnp.float32)
    low = jnp.concatenate([first, tail], axis=0)
    high = pltpu.roll(jnp.concatenate([second, tail], axis=0), count, 0)
    return low + high


def init_kernel(count, half_pairs, meta, signs, panel, send):
    blocks = signs.shape[0]
    width = signs.shape[2]
    pad = jnp.zeros((PAD - count, width), jnp.float32)

    def body(b, carry):
        value = jnp.concatenate([signs[b].astype(jnp.float32), pad], axis=0)
        panel[b] = value.astype(jnp.bfloat16)
        return carry

    lax.fori_loop(0, blocks, body, 0, unroll=8)
    base = meta[1] * (2 * half_pairs)

    def pack(i, carry):
        b = base + 2 * i
        send[i] = join_pair(
            panel[b].astype(jnp.float32), panel[b + 1].astype(jnp.float32), count
        ).astype(jnp.bfloat16)
        return carry

    lax.fori_loop(0, half_pairs, pack, 0, unroll=8)


def init_panel(meta, signs):
    blocks, count, width = signs.shape
    half_pairs = blocks // 4
    return pl.pallas_call(
        functools.partial(init_kernel, count, half_pairs),
        out_shape=(
            jax.ShapeDtypeStruct((blocks, PAD, width), jnp.bfloat16),
            jax.ShapeDtypeStruct((half_pairs, 2 * count, width), jnp.bfloat16),
        ),
        grid_spec=pltpu.PrefetchScalarGridSpec(
            num_scalar_prefetch=1, grid=(1,), in_specs=[whole()], out_specs=(whole(), whole())
        ),
        compiler_params=params(),
        name="init_panel",
    )(meta, signs)


def unpack_kernel(count, where, meta, *refs):
    panel = refs[-1]
    for ref, base_of in zip(refs[:-1], where):
        pairs = ref.shape[0]
        base = base_of(meta[0], meta[1])

        def body(i, carry, ref=ref, base=base):
            first, second = split_pair(ref[i], count)
            panel[base + 2 * i] = first.astype(jnp.bfloat16)
            panel[base + 2 * i + 1] = second.astype(jnp.bfloat16)
            return carry

        lax.fori_loop(0, pairs, body, 0, unroll=8 if pairs % 8 == 0 else 4)


def unpack(meta, pieces, where, blocks):
    count = pieces[0].shape[1] // 2
    width = pieces[0].shape[2]
    return pl.pallas_call(
        functools.partial(unpack_kernel, count, where),
        out_shape=jax.ShapeDtypeStruct((blocks, PAD, width), jnp.bfloat16),
        grid_spec=pltpu.PrefetchScalarGridSpec(
            num_scalar_prefetch=1,
            grid=(1,),
            in_specs=[whole()] * len(pieces),
            out_specs=whole(),
        ),
        compiler_params=params(),
        name="unpack_panel",
    )(meta, *pieces)


def forward_kernel(
    count, chunk, rows, inverse, meta, cols_own, cols_other, own, other, panel, out
):
    half = rows // 2
    step = pl.program_id(0)
    first_own = meta[1] * half + step * chunk
    first_other = step * chunk
    first_block = meta[0] * rows + first_own
    slots = own.shape[1]
    contract = (((1,), (1,)), ((), ()))
    for i in range(0, chunk, 2):
        results = []
        for r in (i, i + 1):
            total = panel[first_block + r].astype(jnp.float32)
            product = None
            for ref, cols, base in ((own, cols_own, first_own), (other, cols_other, first_other)):
                for k in range(slots):
                    term = lax.dot_general(
                        panel[cols[base + r, k]],
                        ref[r, k],
                        contract,
                        preferred_element_type=jnp.float32,
                    )
                    product = term if product is None else product + term
            results.append(total + inverse * product)
        out[i // 2] = join_pair(results[0], results[1], count).astype(jnp.bfloat16)


def forward(meta, cols_own, cols_other, own, other, panel, count, inverse):
    rows, slots, width = own.shape[0], own.shape[1], own.shape[3]
    half = rows // 2
    chunk = min(8, half)
    steps = half // chunk
    block = (chunk, slots, width, width)
    flops = 2 * half * 2 * slots * PAD * width * width
    return pl.pallas_call(
        functools.partial(forward_kernel, count, chunk, rows, inverse),
        out_shape=jax.ShapeDtypeStruct((half // 2, 2 * count, width), jnp.bfloat16),
        grid_spec=pltpu.PrefetchScalarGridSpec(
            num_scalar_prefetch=3,
            grid=(steps,),
            in_specs=[
                pl.BlockSpec(block, lambda g, meta, *_: (meta[1] * steps + g, 0, 0, 0)),
                pl.BlockSpec(block, lambda g, *_: (g, 0, 0, 0)),
                whole(),
            ],
            out_specs=pl.BlockSpec((chunk // 2, 2 * count, width), lambda g, *_: (g, 0, 0)),
        ),
        compiler_params=params(),
        cost_estimate=pl.CostEstimate(
            flops=flops, transcendentals=0, bytes_accessed=2 * half * slots * 2 * width * width
        ),
        name="forward_step",
    )(meta, cols_own, cols_other, own, other, panel)


def backward_kernel(
    count, chunk, rows, meta, cols_own, cols_other, own, other, left, keep, send, total
):
    half = rows // 2
    step = pl.program_id(0)

    @pl.when(step == 0)
    def _():
        total[...] = jnp.zeros_like(total)

    first_own = meta[1] * half + step * chunk
    first_other = step * chunk
    slots = own.shape[1]
    contract = (((1,), (0,)), ((), ()))
    for i in range(0, chunk, 2):
        pair = split_pair(left[step * (chunk // 2) + i // 2], count)
        for r, value in zip((i, i + 1), pair):
            value = value.astype(jnp.bfloat16)
            for ref, cols, base in ((own, cols_own, first_own), (other, cols_other, first_other)):
                for k in range(slots):
                    term = lax.dot_general(
                        value, ref[r, k], contract, preferred_element_type=jnp.float32
                    )
                    target = cols[base + r, k]
                    total[target] = total[target] + term

    @pl.when(step == pl.num_programs(0) - 1)
    def _():
        parts = keep.shape[0]
        for d in range(parts):
            for out, h in ((send, 1), (keep, 0)):
                base = (meta[0] ^ d) * rows + (meta[1] ^ h) * half

                def body(i, carry, out=out, base=base, d=d):
                    out[d, i] = join_pair(
                        total[base + 2 * i], total[base + 2 * i + 1], count
                    ).astype(jnp.bfloat16)
                    return carry

                pairs = half // 2
                lax.fori_loop(0, pairs, body, 0, unroll=8 if pairs % 8 == 0 else 4)


def backward(meta, cols_own, cols_other, own, other, left, blocks):
    rows, slots, width = own.shape[0], own.shape[1], own.shape[3]
    count = left.shape[1] // 2
    half = rows // 2
    chunk = min(8, half)
    steps = half // chunk
    block = (chunk, slots, width, width)
    flops = 2 * half * 2 * slots * PAD * width * width
    result = jax.ShapeDtypeStruct((blocks // rows, half // 2, 2 * count, width), jnp.bfloat16)
    return pl.pallas_call(
        functools.partial(backward_kernel, count, chunk, rows),
        out_shape=(result, result),
        grid_spec=pltpu.PrefetchScalarGridSpec(
            num_scalar_prefetch=3,
            grid=(steps,),
            in_specs=[
                pl.BlockSpec(block, lambda g, meta, *_: (meta[1] * steps + g, 0, 0, 0)),
                pl.BlockSpec(block, lambda g, *_: (g, 0, 0, 0)),
                whole(),
            ],
            out_specs=(whole(), whole()),
            scratch_shapes=[pltpu.VMEM((blocks, PAD, width), jnp.float32)],
        ),
        compiler_params=params(),
        cost_estimate=pl.CostEstimate(
            flops=flops, transcendentals=0, bytes_accessed=2 * half * slots * 2 * width * width
        ),
        name="backward_step",
    )(meta, cols_own, cols_other, own, other, left)


def gradient_kernel(scale, chunk, rows, terms, meta, cols, *refs):
    out = refs[-1]
    lefts = refs[: 4 * terms]
    rights = refs[4 * terms : 8 * terms]
    step = pl.program_id(0)
    slots = out.shape[1]
    contract = (((0,), (0,)), ((), ()))
    for r in range(chunk):
        row = step * chunk + r
        left = []
        for position, ref in enumerate(lefts):
            start = meta[0] * rows if position < terms else 0
            left.append(ref[start + row])
        left = jnp.concatenate(left, axis=0)
        right = []
        for k in range(slots):
            target = cols[row, k]
            right.append(jnp.concatenate([ref[target] for ref in rights], axis=0))
        product = lax.dot_general(
            left, jnp.concatenate(right, axis=1), contract, preferred_element_type=jnp.float32
        )
        width = out.shape[3]
        for k in range(slots):
            out[r, k] = (product[:, k * width : (k + 1) * width] * scale).astype(jnp.bfloat16)


def gradient(meta, cols, lefts, rights, rows, slots, scale):
    width = lefts[0].shape[2]
    chunk = min(8, rows)
    operands = list(lefts) + list(rights)
    return pl.pallas_call(
        functools.partial(gradient_kernel, scale, chunk, rows, len(lefts) // 4),
        out_shape=jax.ShapeDtypeStruct((rows, slots, width, width), jnp.bfloat16),
        grid_spec=pltpu.PrefetchScalarGridSpec(
            num_scalar_prefetch=2,
            grid=(rows // chunk,),
            in_specs=[whole()] * len(operands),
            out_specs=pl.BlockSpec((chunk, slots, width, width), lambda g, *_: (g, 0, 0, 0)),
        ),
        compiler_params=params(),
        name="gradient",
    )(meta, cols, *operands)


def local(block_values, columns, probe_signs):
    rows, slots, width = block_values.shape[0], block_values.shape[1], block_values.shape[3]
    blocks, count = probe_signs.shape[0], probe_signs.shape[1]
    half = rows // 2
    n_var = lax.axis_size("var")
    n_probe = lax.axis_size("probe")
    inverse = 1.0 / math.sqrt(KS * width)
    rep_index = lax.axis_index("rep")
    meta = jnp.stack([lax.axis_index("var"), rep_index]).astype(jnp.int32)

    def swap_rep(x):
        return lax.ppermute(x, "rep", [(0, 1), (1, 0)])

    def shift_var(x, bit):
        return lax.ppermute(x, "var", [(i, i ^ bit) for i in range(n_var)])

    def from_probes(x):
        return [
            lax.ppermute(x, "probe", [(i, (i + d) % n_probe) for i in range(n_probe)])
            for d in range(1, n_probe)
        ]

    bits = [1 << i for i in range(n_var.bit_length() - 1)]

    def gather_var(x):
        held = {0: x}
        for bit in reversed(bits):
            for d in list(held):
                held[d | bit] = shift_var(held[d], bit)
        return [held[d] for d in range(n_var)]

    def scatter_var(parts):
        held = {d: part.astype(jnp.float32) for d, part in enumerate(parts)}
        for bit in bits:
            for d in sorted(held, reverse=True):
                if d & bit:
                    held[d ^ bit] = held[d ^ bit] + shift_var(
                        held.pop(d).astype(jnp.bfloat16), bit
                    ).astype(jnp.float32)
        return held[0]

    start = (1 - rep_index) * half
    other_blocks = swap_rep(lax.dynamic_slice_in_dim(block_values, start, half, 0))
    other_columns = swap_rep(lax.dynamic_slice_in_dim(columns, start, half, 0))

    def home(d, h):
        return lambda v, r: (v ^ d) * rows + (r ^ h) * half

    panel_where = [home(d, 0) for d in range(n_var)] + [home(d, 1) for d in range(n_var)]
    row_where = [lambda v, r: r * half, lambda v, r: (1 - r) * half]

    panel, sent = init_panel(meta, probe_signs)
    right = [[panel]]
    start_where = [lambda v, r: r * (blocks // 2), lambda v, r: (1 - r) * (blocks // 2)]
    for arrived in from_probes(sent):
        right.append([unpack(meta, [arrived, swap_rep(arrived)], start_where, blocks)])
    left = [[group[0]] for group in right]

    def first_rows():
        base = lax.axis_index("var") * rows + rep_index * half
        mine = lax.dynamic_slice_in_dim(probe_signs, base, half, 0)
        return mine.astype(jnp.bfloat16).reshape(half // 2, 2 * count, width)

    left_own = first_rows()
    for step in range(3):
        updated = forward(
            meta, columns, other_columns, block_values, other_blocks, panel, count, inverse
        )
        keep, send = backward(
            meta, columns, other_columns, block_values, other_blocks, left_own, blocks
        )
        pieces = gather_var(updated)
        partner = [swap_rep(x) for x in pieces]
        panel = unpack(meta, pieces + partner, panel_where, blocks)
        right[0].append(panel)
        joined = jnp.concatenate(pieces, axis=0)
        joined_where = panel_where
        for index, arrived in enumerate(from_probes(joined)):
            swapped = swap_rep(arrived)
            size = half // 2
            cut = [arrived[d * size : (d + 1) * size] for d in range(n_var)]
            cut += [swapped[d * size : (d + 1) * size] for d in range(n_var)]
            right[1 + index].append(unpack(meta, cut, joined_where, blocks))

        received = swap_rep(send)
        sums = [
            keep[d].astype(jnp.float32) + received[d].astype(jnp.float32) for d in range(n_var)
        ]
        summed = scatter_var(sums)
        left_own = (left_own.astype(jnp.float32) + inverse * summed).astype(jnp.bfloat16)
        left[0].append(unpack(meta, [left_own, swap_rep(left_own)], row_where, rows))
        for index, arrived in enumerate(from_probes(left_own)):
            left[1 + index].append(
                unpack(meta, [arrived, swap_rep(arrived)], row_where, rows)
            )

    lefts = [group[t] for t in range(4) for group in left]
    rights = [group[3 - t] for t in range(4) for group in right]
    scale = 1.0 / (count * n_probe)
    return gradient(meta, columns, lefts, rights, rows, slots, scale)


def solution(mesh):
    return jax.shard_map(
        local,
        mesh=mesh,
        in_specs=(
            P(("groups", "var"), "rep", None, None),
            P(("groups", "var"), "rep"),
            P("groups", "probe", None),
        ),
        out_specs=P(("groups", "var"), "rep", None, None),
        check_vma=False,
    )
```

```python
import functools
import math

import jax
import jax.numpy as jnp
from jax import lax
from jax.experimental import pallas as pl
from jax.experimental.pallas import tpu as pltpu
from jax.sharding import PartitionSpec as P

KS = 6
PAD = 16
VMEM_LIMIT = 24 * 1024 * 1024


def whole():
    return pl.BlockSpec(memory_space=pltpu.VMEM)


def params():
    return pltpu.CompilerParams(
        dimension_semantics=("arbitrary",), vmem_limit_bytes=VMEM_LIMIT
    )


def split_pair(pair, count):
    wide = pair.astype(jnp.float32)
    keep = lax.broadcasted_iota(jnp.int32, (PAD, wide.shape[1]), 0) < count
    first = jnp.where(keep, wide[:PAD], 0.0)
    second = jnp.where(keep, pltpu.roll(wide, count, 0)[:PAD], 0.0)
    return first, second


def join_pair(first, second, count):
    tail = jnp.zeros((2 * count - PAD, first.shape[1]), jnp.float32)
    low = jnp.concatenate([first, tail], axis=0)
    high = pltpu.roll(jnp.concatenate([second, tail], axis=0), count, 0)
    return low + high


def unpack_kernel(count, where, meta, *refs):
    panel = refs[-1]
    for ref, base_of in zip(refs[:-1], where):
        pairs = ref.shape[0]
        base = base_of(meta[0], meta[1])

        def body(i, carry, ref=ref, base=base):
            first, second = split_pair(ref[i], count)
            panel[base + 2 * i] = first.astype(jnp.bfloat16)
            panel[base + 2 * i + 1] = second.astype(jnp.bfloat16)
            return carry

        lax.fori_loop(0, pairs, body, 0, unroll=8 if pairs % 8 == 0 else 4)


def unpack(meta, pieces, where, blocks):
    count = pieces[0].shape[1] // 2
    width = pieces[0].shape[2]
    return pl.pallas_call(
        functools.partial(unpack_kernel, count, where),
        out_shape=jax.ShapeDtypeStruct((blocks, PAD, width), jnp.bfloat16),
        grid_spec=pltpu.PrefetchScalarGridSpec(
            num_scalar_prefetch=1,
            grid=(1,),
            in_specs=[whole()] * len(pieces),
            out_specs=whole(),
        ),
        compiler_params=params(),
        name="unpack_panel",
    )(meta, *pieces)


def row_product(refs_and_rows, panel, contract):
    picked = []
    stored = []
    for ref, row, cols, col_row in refs_and_rows:
        for k in range(ref.shape[1]):
            picked.append(panel[cols[col_row, k]])
            stored.append(ref[row, k])
    return lax.dot_general(
        jnp.concatenate(picked, axis=1),
        jnp.concatenate(stored, axis=1),
        contract,
        preferred_element_type=jnp.float32,
    )


LAST = (((1,), (1,)), ((), ()))
FIRST = (((1,), (0,)), ((), ()))


def first_forward_kernel(
    count, chunk, meta, cols, signs, stored, panel, sent, keep, send, near, far
):
    step = pl.program_id(0)
    blocks = signs.shape[0]
    half = near.shape[0]

    @pl.when(step == 0)
    def _():
        pad = jnp.zeros((PAD - count, signs.shape[2]), jnp.float32)

        def body(b, carry):
            value = jnp.concatenate([signs[b].astype(jnp.float32), pad], axis=0)
            panel[b] = value.astype(jnp.bfloat16)
            return carry

        lax.fori_loop(0, blocks, body, 0, unroll=8)

    row = step * chunk
    side = row // half
    base = row - side * half
    results = [
        row_product([(stored, r, cols, row + r)], panel, LAST) for r in range(chunk)
    ]
    pairs = [
        join_pair(results[i], results[i + 1], count) for i in range(0, chunk, 2)
    ]

    @pl.when(side == meta[1])
    def _():
        for i, pair in enumerate(pairs):
            keep[base // 2 + i] = pair
        near[pl.ds(base, chunk)] = stored[...]

    @pl.when(side != meta[1])
    def _():
        for i, pair in enumerate(pairs):
            send[base // 2 + i] = pair.astype(jnp.bfloat16)
        far[pl.ds(base, chunk)] = stored[...]

    @pl.when(step == pl.num_programs(0) - 1)
    def _():
        start = meta[1] * (blocks // 2)

        def pack(i, carry):
            b = start + 2 * i
            sent[i] = join_pair(
                panel[b].astype(jnp.float32), panel[b + 1].astype(jnp.float32), count
            ).astype(jnp.bfloat16)
            return carry

        lax.fori_loop(0, blocks // 4, pack, 0, unroll=8)


def first_forward(meta, cols, signs, stored):
    rows, slots, width = stored.shape[0], stored.shape[1], stored.shape[3]
    blocks, count = signs.shape[0], signs.shape[1]
    half = rows // 2
    chunk = min(16, half)
    split = jax.ShapeDtypeStruct((half, slots, width, width), jnp.bfloat16)
    return pl.pallas_call(
        functools.partial(first_forward_kernel, count, chunk),
        out_shape=(
            jax.ShapeDtypeStruct((blocks, PAD, width), jnp.bfloat16),
            jax.ShapeDtypeStruct((blocks // 4, 2 * count, width), jnp.bfloat16),
            jax.ShapeDtypeStruct((half // 2, 2 * count, width), jnp.float32),
            jax.ShapeDtypeStruct((half // 2, 2 * count, width), jnp.bfloat16),
            split,
            split,
        ),
        grid_spec=pltpu.PrefetchScalarGridSpec(
            num_scalar_prefetch=2,
            grid=(rows // chunk,),
            in_specs=[
                whole(),
                pl.BlockSpec((chunk, slots, width, width), lambda g, *_: (g, 0, 0, 0)),
            ],
            out_specs=(whole(),) * 6,
        ),
        compiler_params=params(),
        cost_estimate=cost(rows * slots, width),
        name="first_forward",
    )(meta, cols, signs, stored)


def cost(stored, width):
    return pl.CostEstimate(
        flops=2 * stored * 128 * width * width,
        transcendentals=0,
        bytes_accessed=8 * stored * width * width,
    )


def forward_kernel(count, chunk, rows, inverse, meta, cols_own, cols_other, own, other, panel, out):
    half = rows // 2
    block = meta[0] * rows + meta[1] * half

    def body(step, carry):
        row = step * chunk
        results = []
        for r in range(chunk):
            product = row_product(
                [
                    (own, row + r, cols_own, meta[1] * half + row + r),
                    (other, row + r, cols_other, row + r),
                ],
                panel,
                LAST,
            )
            results.append(panel[block + row + r].astype(jnp.float32) + inverse * product)
        for i in range(0, chunk, 2):
            out[(row + i) // 2] = join_pair(results[i], results[i + 1], count).astype(
                jnp.bfloat16
            )
        return carry

    lax.fori_loop(0, half // chunk, body, 0)


def forward(meta, cols_own, cols_other, own, other, panel, count, inverse):
    half, slots, width = own.shape[0], own.shape[1], own.shape[3]
    chunk = min(16, half)
    return pl.pallas_call(
        functools.partial(forward_kernel, count, chunk, 2 * half, inverse),
        out_shape=jax.ShapeDtypeStruct((half // 2, 2 * count, width), jnp.bfloat16),
        grid_spec=pltpu.PrefetchScalarGridSpec(
            num_scalar_prefetch=3,
            grid=(1,),
            in_specs=[whole()] * 3,
            out_specs=whole(),
        ),
        compiler_params=params(),
        cost_estimate=cost(2 * half * slots, width),
        name="forward_step",
    )(meta, cols_own, cols_other, own, other, panel)


def scatter_row(value, refs_and_rows, total):
    targets = []
    stored = []
    for ref, row, cols, col_row in refs_and_rows:
        for k in range(ref.shape[1]):
            targets.append(cols[col_row, k])
            stored.append(ref[row, k])
    terms = lax.dot_general(
        value, jnp.concatenate(stored, axis=1), FIRST, preferred_element_type=jnp.float32
    )
    width = stored[0].shape[1]
    for i, target in enumerate(targets):
        total[target] = total[target] + terms[:, i * width : (i + 1) * width]


def give_totals(count, rows, meta, keep, send, total):
    half = rows // 2
    pairs = half // 2
    for out, h in ((send, 1), (keep, 0)):
        for d in range(keep.shape[0]):
            base = (meta[0] ^ d) * rows + (meta[1] ^ h) * half

            def body(i, carry, out=out, base=base, d=d):
                out[d, i] = join_pair(
                    total[base + 2 * i], total[base + 2 * i + 1], count
                ).astype(jnp.bfloat16)
                return carry

            lax.fori_loop(0, pairs, body, 0, unroll=8 if pairs % 8 == 0 else 4)


def first_backward_kernel(count, chunk, meta, cols, near, far, panel, keep, send, total):
    half = near.shape[0]
    total[...] = jnp.zeros_like(total)

    def body(step, carry):
        for r in range(chunk):
            for ref, side in ((near, meta[1]), (far, 1 - meta[1])):
                row = step * chunk + r
                place = side * half + row
                value = panel[meta[0] * 2 * half + place]
                scatter_row(value, [(ref, row, cols, place)], total)
        return carry

    lax.fori_loop(0, half // chunk, body, 0)
    give_totals(count, 2 * half, meta, keep, send, total)


def backward_kernel(
    count, chunk, meta, cols_own, cols_other, own, other, left, keep, send, total
):
    half = own.shape[0]
    total[...] = jnp.zeros_like(total)

    def body(step, carry):
        for i in range(0, chunk, 2):
            pair = split_pair(left[(step * chunk + i) // 2], count)
            for r, value in zip((i, i + 1), pair):
                row = step * chunk + r
                scatter_row(
                    value.astype(jnp.bfloat16),
                    [(own, row, cols_own, meta[1] * half + row), (other, row, cols_other, row)],
                    total,
                )
        return carry

    lax.fori_loop(0, half // chunk, body, 0)
    give_totals(count, 2 * half, meta, keep, send, total)


def backward(kernel, name, scalars, own, other, source, count, blocks):
    half, slots, width = own.shape[0], own.shape[1], own.shape[3]
    chunk = min(16, half)
    result = jax.ShapeDtypeStruct(
        (blocks // (2 * half), half // 2, 2 * count, width), jnp.bfloat16
    )
    return pl.pallas_call(
        functools.partial(kernel, count, chunk),
        out_shape=(result, result),
        grid_spec=pltpu.PrefetchScalarGridSpec(
            num_scalar_prefetch=len(scalars),
            grid=(1,),
            in_specs=[whole()] * 3,
            out_specs=(whole(), whole()),
            scratch_shapes=[pltpu.VMEM((blocks, PAD, width), jnp.float32)],
        ),
        compiler_params=params(),
        cost_estimate=cost(2 * half * slots, width),
        name=name,
    )(*scalars, own, other, source)


def gradient_kernel(scale, chunk, rows, terms, meta, cols, *refs):
    out = refs[-1]
    lefts = refs[: 4 * terms]
    rights = refs[4 * terms : 8 * terms]
    step = pl.program_id(0)
    slots = out.shape[1]
    contract = (((0,), (0,)), ((), ()))
    for r in range(chunk):
        row = step * chunk + r
        left = []
        for position, ref in enumerate(lefts):
            start = meta[0] * rows if position < terms else 0
            left.append(ref[start + row])
        left = jnp.concatenate(left, axis=0)
        right = []
        for k in range(slots):
            target = cols[row, k]
            right.append(jnp.concatenate([ref[target] for ref in rights], axis=0))
        product = lax.dot_general(
            left, jnp.concatenate(right, axis=1), contract, preferred_element_type=jnp.float32
        )
        width = out.shape[3]
        for k in range(slots):
            out[r, k] = (product[:, k * width : (k + 1) * width] * scale).astype(jnp.bfloat16)


def gradient(meta, cols, lefts, rights, rows, slots, scale):
    width = lefts[0].shape[2]
    chunk = min(16, rows)
    operands = list(lefts) + list(rights)
    return pl.pallas_call(
        functools.partial(gradient_kernel, scale, chunk, rows, len(lefts) // 4),
        out_shape=jax.ShapeDtypeStruct((rows, slots, width, width), jnp.bfloat16),
        grid_spec=pltpu.PrefetchScalarGridSpec(
            num_scalar_prefetch=2,
            grid=(rows // chunk,),
            in_specs=[whole()] * len(operands),
            out_specs=pl.BlockSpec((chunk, slots, width, width), lambda g, *_: (g, 0, 0, 0)),
        ),
        compiler_params=params(),
        name="gradient",
    )(meta, cols, *operands)


def after(x, *tokens):
    return lax.optimization_barrier((x,) + tokens)[0]


def local(block_values, columns, probe_signs):
    rows, slots, width = block_values.shape[0], block_values.shape[1], block_values.shape[3]
    blocks, count = probe_signs.shape[0], probe_signs.shape[1]
    half = rows // 2
    n_var = lax.axis_size("var")
    n_probe = lax.axis_size("probe")
    inverse = 1.0 / math.sqrt(KS * width)
    rep_index = lax.axis_index("rep")
    meta = jnp.stack([lax.axis_index("var"), rep_index]).astype(jnp.int32)

    def swap_rep(x):
        return lax.ppermute(x, "rep", [(0, 1), (1, 0)])

    def shift_var(x, bit):
        return lax.ppermute(x, "var", [(i, i ^ bit) for i in range(n_var)])

    def from_probes(x):
        return [
            lax.ppermute(x, "probe", [(i, (i + d) % n_probe) for i in range(n_probe)])
            for d in range(1, n_probe)
        ]

    bits = [1 << i for i in range(n_var.bit_length() - 1)]

    def gather_var(x):
        held = {0: x}
        for bit in reversed(bits):
            for d in list(held):
                held[d | bit] = shift_var(held[d], bit)
        return [held[d] for d in range(n_var)]

    def scatter_var(parts):
        held = {d: part.astype(jnp.float32) for d, part in enumerate(parts)}
        for bit in bits:
            for d in sorted(held, reverse=True):
                if d & bit:
                    held[d ^ bit] = held[d ^ bit] + shift_var(
                        held.pop(d).astype(jnp.bfloat16), bit
                    ).astype(jnp.float32)
        return held[0]

    def home(d, h):
        return lambda v, r: (v ^ d) * rows + (r ^ h) * half

    near_where = [home(d, 0) for d in range(n_var)]
    far_where = [home(d, 1) for d in range(n_var)]
    row_where = [lambda v, r: r * half, lambda v, r: (1 - r) * half]
    start_where = [lambda v, r: r * (blocks // 2), lambda v, r: (1 - r) * (blocks // 2)]

    other_columns = swap_rep(
        lax.dynamic_slice_in_dim(columns, (1 - rep_index) * half, half, 0)
    )
    base = lax.axis_index("var") * rows + rep_index * half
    own_signs = lax.dynamic_slice_in_dim(probe_signs, base, half, 0)
    own_signs = own_signs.astype(jnp.bfloat16).reshape(half // 2, 2 * count, width)

    panel, sent, kept, given, near, far = first_forward(
        meta, columns, probe_signs, block_values
    )
    groups = n_probe
    right = [[panel]] + [[] for _ in range(groups - 1)]
    left = [[panel]] + [[] for _ in range(groups - 1)]
    product = kept + swap_rep(given).astype(jnp.float32)
    updated = (own_signs.astype(jnp.float32) + inverse * product).astype(jnp.bfloat16)

    far = after(far, updated)
    other_blocks = swap_rep(far)
    source = after(panel, updated)
    sent = after(sent, updated)
    waiting = [("start", from_probes(sent))]
    left_own = own_signs

    for step in range(3):
        last = step == 2
        if step == 0:
            keep, send = backward(
                first_backward_kernel, "first_backward", (meta, columns), near, far, source,
                count, blocks,
            )
        else:
            keep, send = backward(
                backward_kernel, "backward_step", (meta, columns, other_columns), near,
                other_blocks, after(left_own, updated), count, blocks,
            )
        pieces = gather_var(updated)
        partner = [swap_rep(x) for x in pieces]
        received = swap_rep(send)
        sums = [
            keep[d].astype(jnp.float32) + received[d].astype(jnp.float32) for d in range(n_var)
        ]
        summed = scatter_var(sums)
        panel = unpack(meta, pieces + partner, near_where + far_where, blocks)
        right[0].append(panel)
        for kind, arrays in waiting:
            for index, arrived in enumerate(arrays):
                arrived = after(arrived, keep)
                swapped = swap_rep(arrived)
                if kind == "start":
                    value = unpack(meta, [arrived, swapped], start_where, blocks)
                    left[1 + index].append(value)
                    right[1 + index].append(value)
                elif kind == "right":
                    size = half // 2
                    cut = [arrived[d * size : (d + 1) * size] for d in range(n_var)]
                    cut += [swapped[d * size : (d + 1) * size] for d in range(n_var)]
                    right[1 + index].append(unpack(meta, cut, near_where + far_where, blocks))
                else:
                    left[1 + index].append(
                        unpack(meta, [arrived, swapped], row_where, rows)
                    )
        if not last:
            updated = forward(
                meta, columns, other_columns, near, other_blocks, panel, count, inverse
            )
            joined = after(jnp.concatenate(pieces, axis=0), updated)
            waiting = [("right", from_probes(joined))]
        left_own = (left_own.astype(jnp.float32) + inverse * summed).astype(jnp.bfloat16)
        left[0].append(unpack(meta, [left_own, swap_rep(left_own)], row_where, rows))
        if not last:
            waiting.append(("left", from_probes(left_own)))

    arrived = [from_probes(piece) for piece in pieces]
    for index in range(groups - 1):
        mine = [arrived[d][index] for d in range(n_var)]
        theirs = [swap_rep(x) for x in mine]
        right[1 + index].append(unpack(meta, mine + theirs, near_where + far_where, blocks))
    for index, mine in enumerate(from_probes(left_own)):
        left[1 + index].append(unpack(meta, [mine, swap_rep(mine)], row_where, rows))

    lefts = [group[t] for t in range(4) for group in left]
    rights = [group[3 - t] for t in range(4) for group in right]
    scale = 1.0 / (count * n_probe)
    return gradient(meta, columns, lefts, rights, rows, slots, scale)


def solution(mesh):
    return jax.shard_map(
        local,
        mesh=mesh,
        in_specs=(
            P(("groups", "var"), "rep", None, None),
            P(("groups", "var"), "rep"),
            P("groups", "probe", None),
        ),
        out_specs=P(("groups", "var"), "rep", None, None),
        check_vma=False,
    )
```

```python
import functools
import math

import jax
import jax.numpy as jnp
from jax import lax
from jax.experimental import pallas as pl
from jax.experimental.pallas import tpu as pltpu
from jax.sharding import PartitionSpec as P

KS = 6
PAD = 16
VMEM_LIMIT = 24 * 1024 * 1024


def whole():
    return pl.BlockSpec(memory_space=pltpu.VMEM)


def params():
    return pltpu.CompilerParams(
        dimension_semantics=("arbitrary",), vmem_limit_bytes=VMEM_LIMIT
    )


def split_pair(pair, count):
    wide = pair.astype(jnp.float32)
    keep = lax.broadcasted_iota(jnp.int32, (PAD, wide.shape[1]), 0) < count
    first = jnp.where(keep, wide[:PAD], 0.0)
    second = jnp.where(keep, pltpu.roll(wide, count, 0)[:PAD], 0.0)
    return first, second


def join_pair(first, second, count):
    tail = jnp.zeros((2 * count - PAD, first.shape[1]), jnp.float32)
    low = jnp.concatenate([first, tail], axis=0)
    high = pltpu.roll(jnp.concatenate([second, tail], axis=0), count, 0)
    return low + high


def unpack_kernel(count, where, meta, *refs):
    panel = refs[-1]
    for ref, places in zip(refs[:-1], where):
        pairs = ref.shape[1]
        for index, base_of in enumerate(places):
            if base_of is None:
                continue
            base = base_of(meta[0], meta[1])

            def body(i, carry, ref=ref, base=base, index=index):
                first, second = split_pair(ref[index, i], count)
                panel[base + 2 * i] = first.astype(jnp.bfloat16)
                panel[base + 2 * i + 1] = second.astype(jnp.bfloat16)
                return carry

            lax.fori_loop(0, pairs, body, 0, unroll=8 if pairs % 8 == 0 else 4)


def unpack(meta, pieces, blocks):
    arrays = [array for array, _ in pieces]
    where = [places for _, places in pieces]
    count = arrays[0].shape[2] // 2
    width = arrays[0].shape[3]
    return pl.pallas_call(
        functools.partial(unpack_kernel, count, where),
        out_shape=jax.ShapeDtypeStruct((blocks, PAD, width), jnp.bfloat16),
        grid_spec=pltpu.PrefetchScalarGridSpec(
            num_scalar_prefetch=1,
            grid=(1,),
            in_specs=[whole()] * len(arrays),
            out_specs=whole(),
        ),
        compiler_params=params(),
        name="unpack_panel",
    )(meta, *arrays)


def row_product(refs_and_rows, panel, contract):
    picked = []
    stored = []
    for ref, row, cols, col_row in refs_and_rows:
        for k in range(ref.shape[1]):
            picked.append(panel[cols[k, col_row]])
            stored.append(ref[row, k])
    return lax.dot_general(
        jnp.concatenate(picked, axis=1),
        jnp.concatenate(stored, axis=1),
        contract,
        preferred_element_type=jnp.float32,
    )


LAST = (((1,), (1,)), ((), ()))
FIRST = (((1,), (0,)), ((), ()))


def first_kernel(
    count, chunk, blocks, meta, cols, signs, stored,
    panel, sent, mine, keep_row, near, far, keep, send, total,
):
    step = pl.program_id(0)
    half = near.shape[0]
    rows = 2 * half

    @pl.when(step == 0)
    def _():
        total[...] = jnp.zeros_like(total)
        pad = jnp.zeros((PAD - count, signs.shape[1]), jnp.float32)

        def body(b, carry):
            value = signs[pl.ds(b, count, stride=blocks), :].astype(jnp.float32)
            panel[b] = jnp.concatenate([value, pad], axis=0).astype(jnp.bfloat16)
            return carry

        lax.fori_loop(0, blocks, body, 0, unroll=8)

    row = step * chunk
    side = row // half
    base = row - side * half
    first_block = meta[0] * rows
    pairs = []
    for i in range(0, chunk, 2):
        results = [
            row_product([(stored, r, cols, row + r)], panel, LAST) for r in (i, i + 1)
        ]
        pairs.append(join_pair(results[0], results[1], count))
    for r in range(chunk):
        scatter_row(panel[first_block + row + r], [(stored, r, cols, row + r)], total)

    @pl.when(side == meta[1])
    def _():
        for i, pair in enumerate(pairs):
            keep_row[base // 2 + i] = pair
        near[pl.ds(base, chunk)] = stored[...]

    @pl.when(side != meta[1])
    def _():
        for i, pair in enumerate(pairs):
            send[send.shape[0] - 1, base // 2 + i] = pair.astype(jnp.bfloat16)
        far[pl.ds(base, chunk)] = stored[...]

    @pl.when(step == pl.num_programs(0) - 1)
    def _():
        parts, pair_rows = sent.shape[0], sent.shape[1]
        for start, out, index in [
            (meta[1] * (blocks // 2) + p * 2 * pair_rows, sent, p) for p in range(parts)
        ] + [(first_block + meta[1] * half, mine, 0)]:

            def pack(i, carry, start=start, out=out, index=index):
                b = start + 2 * i
                out[index, i] = join_pair(
                    panel[b].astype(jnp.float32), panel[b + 1].astype(jnp.float32), count
                ).astype(jnp.bfloat16)
                return carry

            lax.fori_loop(0, pair_rows, pack, 0, unroll=8 if pair_rows % 8 == 0 else 4)
        give_totals(count, rows, meta, keep, send, total)


def first_step(meta, cols, signs, stored, blocks):
    rows, slots, width = stored.shape[0], stored.shape[1], stored.shape[3]
    count = signs.shape[0] // blocks
    half = rows // 2
    chunk = min(16, half)
    parts = blocks // rows
    shape = jax.ShapeDtypeStruct
    piece = (half // 2, 2 * count, width)
    return pl.pallas_call(
        functools.partial(first_kernel, count, chunk, blocks),
        out_shape=(
            shape((blocks, PAD, width), jnp.bfloat16),
            shape((parts,) + piece, jnp.bfloat16),
            shape((1,) + piece, jnp.bfloat16),
            shape(piece, jnp.float32),
            shape((half, slots, width, width), jnp.bfloat16),
            shape((half, slots, width, width), jnp.bfloat16),
            shape((parts,) + piece, jnp.bfloat16),
            shape((parts + 1,) + piece, jnp.bfloat16),
        ),
        grid_spec=pltpu.PrefetchScalarGridSpec(
            num_scalar_prefetch=2,
            grid=(rows // chunk,),
            in_specs=[
                whole(),
                pl.BlockSpec((chunk, slots, width, width), lambda g, *_: (g, 0, 0, 0)),
            ],
            out_specs=(whole(),) * 8,
            scratch_shapes=[pltpu.VMEM((blocks, PAD, width), jnp.float32)],
        ),
        compiler_params=params(),
        cost_estimate=cost(2 * rows * slots, width),
        name="first_step",
    )(meta, cols, signs, stored)


def cost(stored, width):
    return pl.CostEstimate(
        flops=2 * stored * 128 * width * width,
        transcendentals=0,
        bytes_accessed=8 * stored * width * width,
    )


def forward_kernel(
    count, chunk, rows, inverse, meta, cols_own, cols_other, own, other, panel, *rest
):
    out = rest[-1]
    half = rows // 2
    block = meta[0] * rows + meta[1] * half

    def body(step, carry):
        row = step * chunk
        for i in range(0, chunk, 2):
            results = []
            for r in (i, i + 1):
                product = row_product(
                    [
                        (own, row + r, cols_own, meta[1] * half + row + r),
                        (other, row + r, cols_other, row + r),
                    ],
                    panel,
                    LAST,
                )
                results.append(panel[block + row + r].astype(jnp.float32) + inverse * product)
            out[0, (row + i) // 2] = join_pair(results[0], results[1], count).astype(
                jnp.bfloat16
            )
        return carry

    lax.fori_loop(0, half // chunk, body, 0)


def forward(meta, cols_own, cols_other, own, other, panel, count, inverse, tokens):
    half, slots, width = own.shape[0], own.shape[1], own.shape[3]
    chunk = min(16, half)
    return pl.pallas_call(
        functools.partial(forward_kernel, count, chunk, 2 * half, inverse),
        out_shape=jax.ShapeDtypeStruct((1, half // 2, 2 * count, width), jnp.bfloat16),
        grid_spec=pltpu.PrefetchScalarGridSpec(
            num_scalar_prefetch=3,
            grid=(1,),
            in_specs=[whole()] * 3 + [pl.BlockSpec(memory_space=pl.ANY)] * len(tokens),
            out_specs=whole(),
        ),
        compiler_params=params(),
        cost_estimate=cost(2 * half * slots, width),
        name="forward_step",
    )(meta, cols_own, cols_other, own, other, panel, *tokens)


def scatter_row(value, refs_and_rows, total):
    targets = []
    stored = []
    for ref, row, cols, col_row in refs_and_rows:
        for k in range(ref.shape[1]):
            targets.append(cols[k, col_row])
            stored.append(ref[row, k])
    terms = lax.dot_general(
        value, jnp.concatenate(stored, axis=1), FIRST, preferred_element_type=jnp.float32
    )
    width = stored[0].shape[1]
    for i, target in enumerate(targets):
        total[target] = total[target] + terms[:, i * width : (i + 1) * width]


def give_totals(count, rows, meta, keep, send, total):
    half = rows // 2
    pairs = half // 2
    for out, h in ((send, 1), (keep, 0)):
        for d in range(keep.shape[0]):
            base = (meta[0] ^ d) * rows + (meta[1] ^ h) * half

            def body(i, carry, out=out, base=base, d=d):
                out[d, i] = join_pair(
                    total[base + 2 * i], total[base + 2 * i + 1], count
                ).astype(jnp.bfloat16)
                return carry

            lax.fori_loop(0, pairs, body, 0, unroll=8 if pairs % 8 == 0 else 4)


def backward_kernel(
    count, chunk, meta, cols_own, cols_other, own, other, left, keep, send, total
):
    half = own.shape[0]
    total[...] = jnp.zeros_like(total)

    def body(step, carry):
        for i in range(0, chunk, 2):
            pair = split_pair(left[0, (step * chunk + i) // 2], count)
            for r, value in zip((i, i + 1), pair):
                row = step * chunk + r
                scatter_row(
                    value.astype(jnp.bfloat16),
                    [(own, row, cols_own, meta[1] * half + row), (other, row, cols_other, row)],
                    total,
                )
        return carry

    lax.fori_loop(0, half // chunk, body, 0)
    give_totals(count, 2 * half, meta, keep, send, total)


def backward(meta, cols_own, cols_other, own, other, left, blocks):
    half, slots, width = own.shape[0], own.shape[1], own.shape[3]
    count = left.shape[2] // 2
    chunk = min(16, half)
    result = jax.ShapeDtypeStruct(
        (blocks // (2 * half), half // 2, 2 * count, width), jnp.bfloat16
    )
    return pl.pallas_call(
        functools.partial(backward_kernel, count, chunk),
        out_shape=(result, result),
        grid_spec=pltpu.PrefetchScalarGridSpec(
            num_scalar_prefetch=3,
            grid=(1,),
            in_specs=[whole()] * 3,
            out_specs=(whole(), whole()),
            scratch_shapes=[pltpu.VMEM((blocks, PAD, width), jnp.float32)],
        ),
        compiler_params=params(),
        cost_estimate=cost(2 * half * slots, width),
        name="backward_step",
    )(meta, cols_own, cols_other, own, other, left)


def gradient_kernel(scale, chunk, rows, terms, meta, cols, *refs):
    out = refs[-1]
    lefts = refs[: 4 * terms]
    rights = refs[4 * terms : 8 * terms]
    step = pl.program_id(0)
    slots = out.shape[1]
    contract = (((0,), (0,)), ((), ()))
    for r in range(chunk):
        row = step * chunk + r
        left = []
        for position, ref in enumerate(lefts):
            start = meta[0] * rows if position < terms else 0
            left.append(ref[start + row])
        left = jnp.concatenate(left, axis=0)
        right = []
        for k in range(slots):
            target = cols[k, row]
            right.append(jnp.concatenate([ref[target] for ref in rights], axis=0))
        product = lax.dot_general(
            left, jnp.concatenate(right, axis=1), contract, preferred_element_type=jnp.float32
        )
        width = out.shape[3]
        for k in range(slots):
            out[r, k] = (product[:, k * width : (k + 1) * width] * scale).astype(jnp.bfloat16)


def gradient(meta, cols, lefts, rights, rows, slots, scale):
    width = lefts[0].shape[2]
    chunk = min(16, rows)
    operands = list(lefts) + list(rights)
    return pl.pallas_call(
        functools.partial(gradient_kernel, scale, chunk, rows, len(lefts) // 4),
        out_shape=jax.ShapeDtypeStruct((rows, slots, width, width), jnp.bfloat16),
        grid_spec=pltpu.PrefetchScalarGridSpec(
            num_scalar_prefetch=2,
            grid=(rows // chunk,),
            in_specs=[whole()] * len(operands),
            out_specs=pl.BlockSpec((chunk, slots, width, width), lambda g, *_: (g, 0, 0, 0)),
        ),
        compiler_params=params(),
        name="gradient",
    )(meta, cols, *operands)


def local(block_values, columns, probe_signs):
    rows, slots, width = block_values.shape[0], block_values.shape[1], block_values.shape[3]
    blocks, count = probe_signs.shape[0], probe_signs.shape[1]
    half = rows // 2
    n_var = lax.axis_size("var")
    n_probe = lax.axis_size("probe")
    inverse = 1.0 / math.sqrt(KS * width)
    rep_index = lax.axis_index("rep")
    meta = jnp.stack([lax.axis_index("var"), rep_index]).astype(jnp.int32)
    signs = jnp.transpose(probe_signs, (1, 0, 2)).reshape(count * blocks, width)
    cols = columns.T

    def swap_rep(x):
        return lax.ppermute(x, "rep", [(0, 1), (1, 0)])

    def shift_var(x, bit):
        return lax.ppermute(x, "var", [(i, i ^ bit) for i in range(n_var)])

    def from_probes(x):
        return jnp.concatenate(
            [
                lax.ppermute(x, "probe", [(i, (i + d) % n_probe) for i in range(n_probe)])
                for d in range(1, n_probe)
            ],
            axis=0,
        )

    def wide(x):
        return x.astype(jnp.float32)

    def narrow(x):
        return x.astype(jnp.bfloat16)

    def exchange(own, parts, extra):
        size = extra.shape[0]
        if n_var == 4:
            far = shift_var(own, 2)
            near = shift_var(jnp.concatenate([own, narrow(parts[3])], axis=0), 1)
            own_other = swap_rep(own)
            crossed = shift_var(narrow(parts[2] + wide(near[1:])), 2)
            last = shift_var(jnp.concatenate([far, narrow(parts[1])], axis=0), 1)
            swapped = swap_rep(jnp.concatenate([near[:1], far, extra], axis=0))
            summed = parts[0] + wide(last[1:]) + wide(crossed)
            pieces = [
                (own, [0]), (near, [1, None]), (far, [2]), (last, [3, None]),
            ]
            others = [
                (own_other, [0]), (swapped, [1, 2] + [None] * size), (swap_rep(last[:1]), [3]),
            ]
            return pieces, others, summed, swapped[2:]
        bits = [1 << i for i in range(n_var.bit_length() - 1)]
        held = {0: own}
        for bit in reversed(bits):
            for d in list(held):
                held[d | bit] = shift_var(held[d], bit)
        sums = dict(enumerate(parts))
        for bit in bits:
            for d in sorted(sums, reverse=True):
                if d & bit:
                    sums[d ^ bit] = sums[d ^ bit] + wide(shift_var(narrow(sums.pop(d)), bit))
        pieces = [(jnp.concatenate([held[d] for d in range(n_var)], axis=0), list(range(n_var)))]
        swapped = swap_rep(jnp.concatenate([pieces[0][0], extra], axis=0))
        others = [(swapped, list(range(n_var)) + [None] * size)]
        return pieces, others, sums[0], swapped[n_var:]

    def home(d, h):
        if d is None:
            return None
        return lambda v, r: (v ^ d) * rows + (r ^ h) * half

    def place(pieces, h):
        return [(array, [home(d, h) for d in ds]) for array, ds in pieces]

    def joined(pieces):
        found = {}
        for array, ds in pieces:
            for i, d in enumerate(ds):
                if d is not None:
                    found[d] = array if len(ds) == 1 else array[i : i + 1]
        return jnp.concatenate([found[d] for d in range(n_var)], axis=0)

    def row_place(h):
        return lambda v, r: (r ^ h) * half

    def sign_place(p, h):
        return lambda v, r: (r ^ h) * (blocks // 2) + p * half

    other_columns = swap_rep(
        lax.dynamic_slice_in_dim(cols, (1 - rep_index) * half, half, 1)
    )
    panel, sent, left_own, kept, near, far, keep, send = first_step(
        meta, cols, signs, block_values, blocks
    )
    received = swap_rep(send)
    other = swap_rep(far)
    updated = narrow(wide(left_own) + inverse * (kept + wide(received[n_var]))[None])
    groups = n_probe - 1
    right = [[panel]] + [[] for _ in range(groups)]
    left = [[panel]] + [[] for _ in range(groups)]
    travelling = from_probes(sent)

    for step in range(3):
        last = step == 2
        parts = [wide(keep[d : d + 1]) + wide(received[d : d + 1]) for d in range(n_var)]
        extra = travelling if step == 0 else jnp.concatenate([travelling, left_own], axis=0)
        pieces, others, summed, extra_other = exchange(updated, parts, extra)
        size = n_var if step == 0 else n_var + 1
        fresh = []
        for index in range(groups):
            spots = {}
            for h in (0, 1):
                where = [None] * extra.shape[0]
                for p in range(n_var):
                    where[index * size + p] = sign_place(p, h) if step == 0 else home(p, h)
                spots[h] = where
            value = unpack(meta, [(travelling, spots[0][: travelling.shape[0]]), (extra_other, spots[1])], blocks)
            right[1 + index].append(value)
            fresh.append(value)
            if step == 0:
                left[1 + index].append(value)
            else:
                spots = {}
                for h in (0, 1):
                    where = [None] * extra.shape[0]
                    where[index * size + n_var] = row_place(h)
                    spots[h] = where
                value = unpack(meta, [(travelling, spots[0][: travelling.shape[0]]), (extra_other, spots[1])], rows)
                left[1 + index].append(value)
                fresh.append(value)
        if step > 0:
            tail = [None] * (extra.shape[0] - 1)
            value = unpack(
                meta, [(left_own, [row_place(0)]), (extra_other, tail + [row_place(1)])], rows
            )
            left[0].append(value)
            fresh.append(value)
        panel = unpack(meta, place(pieces, 0) + place(others, 1), blocks)
        right[0].append(panel)
        left_own = narrow(wide(left_own) + inverse * summed)
        if not last:
            travelling = from_probes(jnp.concatenate([joined(pieces), left_own], axis=0))
            keep, send = backward(meta, cols, other_columns, near, other, left_own, blocks)
            received = swap_rep(send)
            updated = forward(
                meta, cols, other_columns, near, other, panel, count, inverse, [send] + fresh
            )

    if n_var == 4:
        first = from_probes(jnp.concatenate([pieces[0][0], pieces[1][0][:1], pieces[2][0]], axis=0))
        late = from_probes(jnp.concatenate([pieces[3][0][:1], left_own], axis=0))
        arrays = [(first, [0, 1, 2]), (late, [3, "row"])]
    else:
        arrays = [(from_probes(jnp.concatenate([joined(pieces), left_own], axis=0)), list(range(n_var)) + ["row"])]
    crossed = [swap_rep(array) for array, _ in arrays]
    for index in range(groups):
        blocks_in = []
        rows_in = []
        for h, versions in ((0, [array for array, _ in arrays]), (1, crossed)):
            for array, (_, ds) in zip(versions, arrays):
                lead = [None] * (index * len(ds))
                rest = [None] * (array.shape[0] - (index + 1) * len(ds))
                here = [None if d == "row" else home(d, h) for d in ds]
                blocks_in.append((array, lead + here + rest))
                if "row" in ds:
                    here = [row_place(h) if d == "row" else None for d in ds]
                    rows_in.append((array, lead + here + rest))
        right[1 + index].append(unpack(meta, blocks_in, blocks))
        left[1 + index].append(unpack(meta, rows_in, rows))
    left[0].append(
        unpack(meta, [(left_own, [row_place(0)]), (swap_rep(left_own), [row_place(1)])], rows)
    )

    lefts = [group[t] for t in range(4) for group in left]
    rights = [group[3 - t] for t in range(4) for group in right]
    scale = 1.0 / (count * n_probe)
    return gradient(meta, cols, lefts, rights, rows, slots, scale)


def solution(mesh):
    return jax.shard_map(
        local,
        mesh=mesh,
        in_specs=(
            P(("groups", "var"), "rep", None, None),
            P(("groups", "var"), "rep"),
            P("groups", "probe", None),
        ),
        out_specs=P(("groups", "var"), "rep", None, None),
        check_vma=False,
    )
```

```python
import functools
import math

import jax
import jax.numpy as jnp
from jax import lax
from jax.experimental import pallas as pl
from jax.experimental.pallas import tpu as pltpu
from jax.sharding import PartitionSpec as P

KS = 6
PAD = 16
VMEM_LIMIT = 16 * 1024 * 1024


def whole():
    return pl.BlockSpec(memory_space=pltpu.VMEM)


def params():
    return pltpu.CompilerParams(
        dimension_semantics=("arbitrary",), vmem_limit_bytes=VMEM_LIMIT
    )


def split_pair(pair, count):
    wide = pair.astype(jnp.float32)
    keep = lax.broadcasted_iota(jnp.int32, (PAD, wide.shape[1]), 0) < count
    first = jnp.where(keep, wide[:PAD], 0.0)
    second = jnp.where(keep, pltpu.roll(wide, count, 0)[:PAD], 0.0)
    return first, second


def join_pair(first, second, count):
    tail = jnp.zeros((2 * count - PAD, first.shape[1]), jnp.float32)
    low = jnp.concatenate([first, tail], axis=0)
    high = pltpu.roll(jnp.concatenate([second, tail], axis=0), count, 0)
    return low + high


def anywhere():
    return pl.BlockSpec(memory_space=pl.ANY)


def in_hbm():
    return pl.BlockSpec(memory_space=pltpu.HBM)


def unpack_into(panel, refs, where, count, meta):
    for ref, places in zip(refs, where):
        pairs = ref.shape[1]
        for index, base_of in enumerate(places):
            if base_of is None:
                continue
            base = base_of(meta[0], meta[1])

            def body(i, carry, ref=ref, base=base, index=index):
                first, second = split_pair(ref[index, i], count)
                panel[base + 2 * i] = first.astype(jnp.bfloat16)
                panel[base + 2 * i + 1] = second.astype(jnp.bfloat16)
                return carry

            lax.fori_loop(0, pairs, body, 0, unroll=8 if pairs % 8 == 0 else 4)


def unpack_kernel(count, wheres, skipped, meta, *refs):
    panels = refs[len(refs) - len(wheres) :]
    begin = 0
    for panel, where in zip(panels, wheres):
        unpack_into(panel, refs[begin : begin + len(where)], where, count, meta)
        begin += len(where)


def unpack(meta, jobs, tokens=()):
    arrays = [array for pieces, _ in jobs for array, _ in pieces]
    wheres = [[places for _, places in pieces] for pieces, _ in jobs]
    count = arrays[0].shape[2] // 2
    width = arrays[0].shape[3]
    return pl.pallas_call(
        functools.partial(unpack_kernel, count, wheres, len(tokens)),
        out_shape=[
            jax.ShapeDtypeStruct((blocks, PAD, width), jnp.bfloat16) for _, blocks in jobs
        ],
        grid_spec=pltpu.PrefetchScalarGridSpec(
            num_scalar_prefetch=1,
            grid=(1,),
            in_specs=[whole()] * len(arrays) + [anywhere()] * len(tokens),
            out_specs=[whole()] * len(jobs),
        ),
        compiler_params=params(),
        name="unpack_panels",
    )(meta, *arrays, *tokens)


def fetch_kernel(stored, token, out, sem):
    half = out.shape[0]
    start = (1 - lax.axis_index("rep")) * half
    copy = pltpu.make_async_copy(stored.at[pl.ds(start, half)], out, sem)
    copy.start()
    copy.wait()


def fetch_far(stored, token):
    half = stored.shape[0] // 2
    return pl.pallas_call(
        fetch_kernel,
        out_shape=jax.ShapeDtypeStruct((half,) + stored.shape[1:], stored.dtype),
        in_specs=[in_hbm(), anywhere()],
        out_specs=whole(),
        scratch_shapes=[pltpu.SemaphoreType.DMA(())],
        compiler_params=pltpu.CompilerParams(vmem_limit_bytes=VMEM_LIMIT),
        name="fetch_far",
    )(stored, token)


def row_product(refs_and_rows, panel, contract):
    picked = []
    stored = []
    for ref, row, cols, col_row in refs_and_rows:
        for k in range(ref.shape[1]):
            picked.append(panel[cols[k, col_row]])
            stored.append(ref[row, k])
    return lax.dot_general(
        jnp.concatenate(picked, axis=1),
        jnp.concatenate(stored, axis=1),
        contract,
        preferred_element_type=jnp.float32,
    )


LAST = (((1,), (1,)), ((), ()))
FIRST = (((1,), (0,)), ((), ()))


def first_kernel(
    count, chunk, blocks, meta, cols, signs_hbm, stored,
    panel, sent, mine, keep_row, near, keep, send,
    signs, far, total, sign_sem, sems,
):
    half = near.shape[0]
    rows = 2 * half
    chunks = half // chunk
    rep = lax.axis_index("rep")

    def copy(side, c):
        place = (rep if side == 0 else 1 - rep) * half + c * chunk
        return pltpu.make_async_copy(
            stored.at[pl.ds(place, chunk)],
            (near, far)[side].at[pl.ds(c * chunk, chunk)],
            sems.at[side * chunks + c],
        )

    sign_copy = pltpu.make_async_copy(signs_hbm, signs, sign_sem)
    sign_copy.start()
    for side in (0, 1):
        for c in range(chunks):
            copy(side, c).start()
    total[...] = jnp.zeros_like(total)
    sign_copy.wait()
    pad = jnp.zeros((PAD - count, signs.shape[1]), jnp.float32)

    def convert(b, carry):
        value = signs[pl.ds(b, count, stride=blocks), :].astype(jnp.float32)
        panel[b] = jnp.concatenate([value, pad], axis=0).astype(jnp.bfloat16)
        return carry

    lax.fori_loop(0, blocks, convert, 0, unroll=8)
    first_block = meta[0] * rows
    for side, ref in ((0, near), (1, far)):
        offset = meta[1] * half if side == 0 else (1 - meta[1]) * half

        def body(c, carry, side=side, ref=ref, offset=offset):
            copy(side, c).wait()
            row = c * chunk
            for i in range(0, chunk, 2):
                results = [
                    row_product([(ref, row + r, cols, offset + row + r)], panel, LAST)
                    for r in (i, i + 1)
                ]
                pair = join_pair(results[0], results[1], count)
                if side == 0:
                    keep_row[(row + i) // 2] = pair
                else:
                    send[send.shape[0] - 1, (row + i) // 2] = pair.astype(jnp.bfloat16)
                for r in (i, i + 1):
                    scatter_row(
                        panel[first_block + offset + row + r],
                        [(ref, row + r, cols, offset + row + r)],
                        total,
                    )
            return carry

        lax.fori_loop(0, chunks, body, 0)
    parts, pair_rows = sent.shape[0], sent.shape[1]
    for start, out, index in [
        (meta[1] * (blocks // 2) + p * 2 * pair_rows, sent, p) for p in range(parts)
    ] + [(first_block + meta[1] * half, mine, 0)]:

        def pack(i, carry, start=start, out=out, index=index):
            b = start + 2 * i
            out[index, i] = join_pair(
                panel[b].astype(jnp.float32), panel[b + 1].astype(jnp.float32), count
            ).astype(jnp.bfloat16)
            return carry

        lax.fori_loop(0, pair_rows, pack, 0, unroll=8 if pair_rows % 8 == 0 else 4)
    give_totals(count, rows, meta, keep, send, total)


def first_step(meta, cols, signs, stored, blocks):
    rows, slots, width = stored.shape[0], stored.shape[1], stored.shape[3]
    count = signs.shape[0] // blocks
    half = rows // 2
    chunk = min(16, half)
    parts = blocks // rows
    shape = jax.ShapeDtypeStruct
    piece = (half // 2, 2 * count, width)
    return pl.pallas_call(
        functools.partial(first_kernel, count, chunk, blocks),
        out_shape=(
            shape((blocks, PAD, width), jnp.bfloat16),
            shape((parts,) + piece, jnp.bfloat16),
            shape((1,) + piece, jnp.bfloat16),
            shape(piece, jnp.float32),
            shape((half, slots, width, width), jnp.bfloat16),
            shape((parts,) + piece, jnp.bfloat16),
            shape((parts + 1,) + piece, jnp.bfloat16),
        ),
        grid_spec=pltpu.PrefetchScalarGridSpec(
            num_scalar_prefetch=2,
            grid=(1,),
            in_specs=[in_hbm(), in_hbm()],
            out_specs=(whole(),) * 7,
            scratch_shapes=[
                pltpu.VMEM(signs.shape, jnp.int32),
                pltpu.VMEM((half, slots, width, width), jnp.bfloat16),
                pltpu.VMEM((blocks, PAD, width), jnp.float32),
                pltpu.SemaphoreType.DMA(()),
                pltpu.SemaphoreType.DMA((2 * half // chunk,)),
            ],
        ),
        compiler_params=params(),
        cost_estimate=cost(2 * rows * slots, width),
        name="first_step",
    )(meta, cols, signs, stored)


def cost(stored, width):
    return pl.CostEstimate(
        flops=2 * stored * 128 * width * width,
        transcendentals=0,
        bytes_accessed=8 * stored * width * width,
    )


def forward_kernel(
    count, chunk, rows, inverse, where, meta, cols_own, cols_other, own, other, *rest
):
    panel, out = rest[-2:]
    unpack_into(panel, rest[: len(where)], where, count, meta)
    half = rows // 2
    block = meta[0] * rows + meta[1] * half

    def body(step, carry):
        row = step * chunk
        for i in range(0, chunk, 2):
            results = []
            for r in (i, i + 1):
                product = row_product(
                    [
                        (own, row + r, cols_own, meta[1] * half + row + r),
                        (other, row + r, cols_other, meta[1] * half + row + r),
                    ],
                    panel,
                    LAST,
                )
                results.append(panel[block + row + r].astype(jnp.float32) + inverse * product)
            out[0, (row + i) // 2] = join_pair(results[0], results[1], count).astype(
                jnp.bfloat16
            )
        return carry

    lax.fori_loop(0, half // chunk, body, 0)


def forward(meta, cols_own, cols_other, own, other, pieces, blocks, inverse, tokens):
    half, slots, width = own.shape[0], own.shape[1], own.shape[3]
    arrays = [array for array, _ in pieces]
    count = arrays[0].shape[2] // 2
    chunk = min(16, half)
    return pl.pallas_call(
        functools.partial(
            forward_kernel, count, chunk, 2 * half, inverse, [places for _, places in pieces]
        ),
        out_shape=(
            jax.ShapeDtypeStruct((blocks, PAD, width), jnp.bfloat16),
            jax.ShapeDtypeStruct((1, half // 2, 2 * count, width), jnp.bfloat16),
        ),
        grid_spec=pltpu.PrefetchScalarGridSpec(
            num_scalar_prefetch=3,
            grid=(1,),
            in_specs=[whole()] * (2 + len(arrays)) + [anywhere()] * len(tokens),
            out_specs=(whole(), whole()),
        ),
        compiler_params=params(),
        cost_estimate=cost(2 * half * slots, width),
        name="forward_step",
    )(meta, cols_own, cols_other, own, other, *arrays, *tokens)


def scatter_row(value, refs_and_rows, total):
    targets = []
    stored = []
    for ref, row, cols, col_row in refs_and_rows:
        for k in range(ref.shape[1]):
            targets.append(cols[k, col_row])
            stored.append(ref[row, k])
    terms = lax.dot_general(
        value, jnp.concatenate(stored, axis=1), FIRST, preferred_element_type=jnp.float32
    )
    width = stored[0].shape[1]
    for i, target in enumerate(targets):
        total[target] = total[target] + terms[:, i * width : (i + 1) * width]


def give_totals(count, rows, meta, keep, send, total):
    half = rows // 2
    pairs = half // 2
    for out, h in ((send, 1), (keep, 0)):
        for d in range(keep.shape[0]):
            base = (meta[0] ^ d) * rows + (meta[1] ^ h) * half

            def body(i, carry, out=out, base=base, d=d):
                out[d, i] = join_pair(
                    total[base + 2 * i], total[base + 2 * i + 1], count
                ).astype(jnp.bfloat16)
                return carry

            lax.fori_loop(0, pairs, body, 0, unroll=8 if pairs % 8 == 0 else 4)


def backward_kernel(
    count, chunk, meta, cols_own, cols_other, own, other, left, keep, send, total
):
    half = own.shape[0]
    stored = ((own, cols_own), (other, cols_other))
    total[...] = jnp.zeros_like(total)

    def body(step, carry):
        for i in range(0, chunk, 2):
            pair = split_pair(left[0, (step * chunk + i) // 2], count)
            for r, value in zip((i, i + 1), pair):
                row = step * chunk + r
                scatter_row(
                    value.astype(jnp.bfloat16),
                    [(ref, row, cols, meta[1] * half + row) for ref, cols in stored],
                    total,
                )
        return carry

    lax.fori_loop(0, half // chunk, body, 0)
    give_totals(count, 2 * half, meta, keep, send, total)


def backward(meta, cols_own, cols_other, own, other, left, blocks):
    half, slots, width = own.shape[0], own.shape[1], own.shape[3]
    count = left.shape[2] // 2
    chunk = min(16, half)
    result = jax.ShapeDtypeStruct(
        (blocks // (2 * half), half // 2, 2 * count, width), jnp.bfloat16
    )
    return pl.pallas_call(
        functools.partial(backward_kernel, count, chunk),
        out_shape=(result, result),
        grid_spec=pltpu.PrefetchScalarGridSpec(
            num_scalar_prefetch=3,
            grid=(1,),
            in_specs=[whole()] * 3,
            out_specs=(whole(), whole()),
            scratch_shapes=[pltpu.VMEM((blocks, PAD, width), jnp.float32)],
        ),
        compiler_params=params(),
        cost_estimate=cost(2 * half * slots, width),
        name="backward_step",
    )(meta, cols_own, cols_other, own, other, left)


def gradient_kernel(scale, chunk, rows, terms, meta, cols, *refs):
    out = refs[-1]
    lefts = refs[: 4 * terms]
    rights = refs[4 * terms : 8 * terms]
    step = pl.program_id(0)
    slots = out.shape[1]
    contract = (((0,), (0,)), ((), ()))
    for r in range(chunk):
        row = step * chunk + r
        left = []
        for position, ref in enumerate(lefts):
            start = meta[0] * rows if position < terms else 0
            left.append(ref[start + row])
        left = jnp.concatenate(left, axis=0)
        right = []
        for k in range(slots):
            target = cols[k, row]
            right.append(jnp.concatenate([ref[target] for ref in rights], axis=0))
        product = lax.dot_general(
            left, jnp.concatenate(right, axis=1), contract, preferred_element_type=jnp.float32
        )
        width = out.shape[3]
        for k in range(slots):
            out[r, k] = (product[:, k * width : (k + 1) * width] * scale).astype(jnp.bfloat16)


def gradient(meta, cols, lefts, rights, rows, slots, scale):
    width = lefts[0].shape[2]
    chunk = min(16, rows)
    operands = list(lefts) + list(rights)
    return pl.pallas_call(
        functools.partial(gradient_kernel, scale, chunk, rows, len(lefts) // 4),
        out_shape=jax.ShapeDtypeStruct((rows, slots, width, width), jnp.bfloat16),
        grid_spec=pltpu.PrefetchScalarGridSpec(
            num_scalar_prefetch=2,
            grid=(rows // chunk,),
            in_specs=[whole()] * len(operands),
            out_specs=pl.BlockSpec((chunk, slots, width, width), lambda g, *_: (g, 0, 0, 0)),
        ),
        compiler_params=params(),
        name="gradient",
    )(meta, cols, *operands)


def local(block_values, columns, probe_signs):
    rows, slots, width = block_values.shape[0], block_values.shape[1], block_values.shape[3]
    blocks, count = probe_signs.shape[0], probe_signs.shape[1]
    half = rows // 2
    n_var = lax.axis_size("var")
    n_probe = lax.axis_size("probe")
    inverse = 1.0 / math.sqrt(KS * width)
    rep_index = lax.axis_index("rep")
    meta = jnp.stack([lax.axis_index("var"), rep_index]).astype(jnp.int32)
    signs = jnp.transpose(probe_signs, (1, 0, 2)).reshape(count * blocks, width)
    cols = columns.T
    block_values = pltpu.with_memory_space_constraint(block_values, pltpu.HBM)

    def swap_rep(x):
        return lax.ppermute(x, "rep", [(0, 1), (1, 0)])

    def shift_var(x, bit):
        return lax.ppermute(x, "var", [(i, i ^ bit) for i in range(n_var)])

    def from_probes(x):
        return jnp.concatenate(
            [
                lax.ppermute(x, "probe", [(i, (i + d) % n_probe) for i in range(n_probe)])
                for d in range(1, n_probe)
            ],
            axis=0,
        )

    def wide(x):
        return x.astype(jnp.float32)

    def narrow(x):
        return x.astype(jnp.bfloat16)

    def exchange(own, parts, extra):
        size = extra.shape[0]
        if n_var == 4:
            far = shift_var(own, 2)
            near = shift_var(jnp.concatenate([own, narrow(parts[3])], axis=0), 1)
            own_other = swap_rep(own)
            crossed = shift_var(narrow(parts[2] + wide(near[1:])), 2)
            last = shift_var(jnp.concatenate([far, narrow(parts[1])], axis=0), 1)
            swapped = swap_rep(jnp.concatenate([near[:1], far, extra], axis=0))
            summed = parts[0] + wide(last[1:]) + wide(crossed)
            pieces = [
                (own, [0]), (near, [1, None]), (far, [2]), (last, [3, None]),
            ]
            others = [
                (own_other, [0]), (swapped, [1, 2] + [None] * size), (swap_rep(last[:1]), [3]),
            ]
            return pieces, others, summed, swapped[2:], near
        bits = [1 << i for i in range(n_var.bit_length() - 1)]
        held = {0: own}
        for bit in reversed(bits):
            for d in list(held):
                held[d | bit] = shift_var(held[d], bit)
        sums = dict(enumerate(parts))
        for bit in bits:
            for d in sorted(sums, reverse=True):
                if d & bit:
                    sums[d ^ bit] = sums[d ^ bit] + wide(shift_var(narrow(sums.pop(d)), bit))
        pieces = [(jnp.concatenate([held[d] for d in range(n_var)], axis=0), list(range(n_var)))]
        swapped = swap_rep(jnp.concatenate([pieces[0][0], extra], axis=0))
        others = [(swapped, list(range(n_var)) + [None] * size)]
        return pieces, others, sums[0], swapped[n_var:], own

    def home(d, h):
        if d is None:
            return None
        return lambda v, r: (v ^ d) * rows + (r ^ h) * half

    def place(pieces, h):
        return [(array, [home(d, h) for d in ds]) for array, ds in pieces]

    def joined(pieces):
        found = {}
        for array, ds in pieces:
            for i, d in enumerate(ds):
                if d is not None:
                    found[d] = array if len(ds) == 1 else array[i : i + 1]
        return jnp.concatenate([found[d] for d in range(n_var)], axis=0)

    def row_place(h):
        return lambda v, r: (r ^ h) * half

    def sign_place(p, h):
        return lambda v, r: (r ^ h) * (blocks // 2) + p * half

    other_columns = swap_rep(cols)
    panel, sent, left_own, kept, near, keep, send = first_step(
        meta, cols, signs, block_values, blocks
    )
    received = swap_rep(send)
    updated = narrow(wide(left_own) + inverse * (kept + wide(received[n_var]))[None])
    groups = n_probe - 1
    right = [[panel]] + [[] for _ in range(groups)]
    left = [[panel]] + [[] for _ in range(groups)]
    travelling = from_probes(sent)

    for step in range(3):
        last = step == 2
        parts = [wide(keep[d : d + 1]) + wide(received[d : d + 1]) for d in range(n_var)]
        extra = travelling if step == 0 else jnp.concatenate([travelling, left_own], axis=0)
        pieces, others, summed, extra_other, mark = exchange(updated, parts, extra)
        if step == 0:
            other = swap_rep(fetch_far(block_values, mark))
        size = n_var if step == 0 else n_var + 1
        total = travelling.shape[0]
        jobs = []
        for index in range(groups):

            def spots(h, kind, index=index):
                where = [None] * extra.shape[0]
                for p in range(n_var):
                    if kind == "blocks":
                        where[index * size + p] = sign_place(p, h) if step == 0 else home(p, h)
                if kind == "rows":
                    where[index * size + n_var] = row_place(h)
                return where

            for kind in ("blocks",) if step == 0 else ("blocks", "rows"):
                jobs.append(
                    (
                        [
                            (travelling, spots(0, kind)[:total]),
                            (extra_other, spots(1, kind)),
                        ],
                        blocks if kind == "blocks" else rows,
                    )
                )
        if step > 0:
            tail = [None] * (extra.shape[0] - 1)
            jobs.append(
                ([(left_own, [row_place(0)]), (extra_other, tail + [row_place(1)])], rows)
            )
        fresh = unpack(meta, jobs)
        found = list(fresh)
        for index in range(groups):
            value = found.pop(0)
            right[1 + index].append(value)
            left[1 + index].append(value if step == 0 else found.pop(0))
        if step > 0:
            left[0].append(found.pop(0))
        sources = place(pieces, 0) + place(others, 1)
        left_own = narrow(wide(left_own) + inverse * summed)
        if not last:
            keep, send = backward(meta, cols, other_columns, near, other, left_own, blocks)
            received = swap_rep(send)
            message = jnp.concatenate([joined(pieces), left_own], axis=0)
            panel, updated = forward(
                meta, cols, other_columns, near, other, sources, blocks, inverse,
                [send] + list(fresh),
            )
            right[0].append(panel)
            travelling = from_probes(message)
        else:
            (panel,) = unpack(meta, [(sources, blocks)], fresh)
            right[0].append(panel)

    if n_var == 4:
        arrays = [
            (from_probes(pieces[0][0]), [0]),
            (from_probes(jnp.concatenate([pieces[1][0][:1], pieces[2][0]], axis=0)), [1, 2]),
            (from_probes(jnp.concatenate([pieces[3][0][:1], left_own], axis=0)), [3, "row"]),
        ]
    else:
        arrays = [
            (
                from_probes(jnp.concatenate([joined(pieces), left_own], axis=0)),
                list(range(n_var)) + ["row"],
            )
        ]
    crossed = [swap_rep(array) for array, _ in arrays]
    jobs = []
    for index in range(groups):
        blocks_in = []
        rows_in = []
        for h, versions in ((0, [array for array, _ in arrays]), (1, crossed)):
            for array, (_, ds) in zip(versions, arrays):
                lead = [None] * (index * len(ds))
                rest = [None] * (array.shape[0] - (index + 1) * len(ds))
                here = [None if d == "row" else home(d, h) for d in ds]
                blocks_in.append((array, lead + here + rest))
                if "row" in ds:
                    here = [row_place(h) if d == "row" else None for d in ds]
                    rows_in.append((array, lead + here + rest))
        jobs += [(blocks_in, blocks), (rows_in, rows)]
    jobs.append(([(left_own, [row_place(0)]), (swap_rep(left_own), [row_place(1)])], rows))
    found = unpack(meta, jobs, [panel])
    for index in range(groups):
        right[1 + index].append(found[2 * index])
        left[1 + index].append(found[2 * index + 1])
    left[0].append(found[-1])

    lefts = [group[t] for t in range(4) for group in left]
    rights = [group[3 - t] for t in range(4) for group in right]
    scale = 1.0 / (count * n_probe)
    return gradient(meta, cols, lefts, rights, rows, slots, scale)


def solution(mesh):
    return jax.shard_map(
        local,
        mesh=mesh,
        in_specs=(
            P(("groups", "var"), "rep", None, None),
            P(("groups", "var"), "rep"),
            P("groups", "probe", None),
        ),
        out_specs=P(("groups", "var"), "rep", None, None),
        check_vma=False,
    )
```

```python
import functools
import math

import jax
import jax.numpy as jnp
from jax import lax
from jax.experimental import pallas as pl
from jax.experimental.pallas import tpu as pltpu
from jax.sharding import PartitionSpec as P

KS = 6
PAD = 16
VMEM_LIMIT = 16 * 1024 * 1024


def whole():
    return pl.BlockSpec(memory_space=pltpu.VMEM)


def params():
    return pltpu.CompilerParams(
        dimension_semantics=("arbitrary",), vmem_limit_bytes=VMEM_LIMIT
    )


def split_pair(pair, count):
    wide = pair.astype(jnp.float32)
    keep = lax.broadcasted_iota(jnp.int32, (PAD, wide.shape[1]), 0) < count
    first = jnp.where(keep, wide[:PAD], 0.0)
    second = jnp.where(keep, pltpu.roll(wide, count, 0)[:PAD], 0.0)
    return first, second


def join_pair(first, second, count):
    tail = jnp.zeros((2 * count - PAD, first.shape[1]), jnp.float32)
    low = jnp.concatenate([first, tail], axis=0)
    high = pltpu.roll(jnp.concatenate([second, tail], axis=0), count, 0)
    return low + high


def anywhere():
    return pl.BlockSpec(memory_space=pl.ANY)


def in_hbm():
    return pl.BlockSpec(memory_space=pltpu.HBM)


def unpack_into(panel, refs, where, count, meta):
    for ref, places in zip(refs, where):
        pairs = ref.shape[1]
        for index, base_of in enumerate(places):
            if base_of is None:
                continue
            base = base_of(meta[0], meta[1])

            def body(i, carry, ref=ref, base=base, index=index):
                first, second = split_pair(ref[index, i], count)
                panel[base + 2 * i] = first.astype(jnp.bfloat16)
                panel[base + 2 * i + 1] = second.astype(jnp.bfloat16)
                return carry

            lax.fori_loop(0, pairs, body, 0, unroll=8 if pairs % 8 == 0 else 4)


def unpack_kernel(count, wheres, skipped, meta, *refs):
    panels = refs[len(refs) - len(wheres) :]
    begin = 0
    for panel, where in zip(panels, wheres):
        unpack_into(panel, refs[begin : begin + len(where)], where, count, meta)
        begin += len(where)


def unpack(meta, jobs, tokens=()):
    arrays = [array for pieces, _ in jobs for array, _ in pieces]
    wheres = [[places for _, places in pieces] for pieces, _ in jobs]
    count = arrays[0].shape[2] // 2
    width = arrays[0].shape[3]
    return pl.pallas_call(
        functools.partial(unpack_kernel, count, wheres, len(tokens)),
        out_shape=[
            jax.ShapeDtypeStruct((blocks, PAD, width), jnp.bfloat16) for _, blocks in jobs
        ],
        grid_spec=pltpu.PrefetchScalarGridSpec(
            num_scalar_prefetch=1,
            grid=(1,),
            in_specs=[whole()] * len(arrays) + [anywhere()] * len(tokens),
            out_specs=[whole()] * len(jobs),
        ),
        compiler_params=params(),
        name="unpack_panels",
    )(meta, *arrays, *tokens)


def row_product(refs_and_rows, panel, contract):
    picked = []
    stored = []
    for ref, row, cols, col_row in refs_and_rows:
        for k in range(ref.shape[1]):
            picked.append(panel[cols[k, col_row]])
            stored.append(ref[row, k])
    return lax.dot_general(
        jnp.concatenate(picked, axis=1),
        jnp.concatenate(stored, axis=1),
        contract,
        preferred_element_type=jnp.float32,
    )


LAST = (((1,), (1,)), ((), ()))
FIRST = (((1,), (0,)), ((), ()))


def first_kernel(
    count, chunk, blocks, meta, cols, signs_hbm, stored,
    panel, sent, mine, keep_row, near, far, keep, send,
    signs, total, sign_sem, sems,
):
    half = near.shape[0]
    rows = 2 * half
    chunks = half // chunk
    rep = lax.axis_index("rep")

    def copy(side, c):
        place = (rep if side == 0 else 1 - rep) * half + c * chunk
        return pltpu.make_async_copy(
            stored.at[pl.ds(place, chunk)],
            (near, far)[side].at[pl.ds(c * chunk, chunk)],
            sems.at[side * chunks + c],
        )

    sign_copy = pltpu.make_async_copy(signs_hbm, signs, sign_sem)
    sign_copy.start()
    for side in (0, 1):
        for c in range(chunks):
            copy(side, c).start()
    total[...] = jnp.zeros_like(total)
    sign_copy.wait()
    pad = jnp.zeros((PAD - count, signs.shape[1]), jnp.float32)

    def convert(b, carry):
        value = signs[pl.ds(b, count, stride=blocks), :].astype(jnp.float32)
        panel[b] = jnp.concatenate([value, pad], axis=0).astype(jnp.bfloat16)
        return carry

    lax.fori_loop(0, blocks, convert, 0, unroll=8)
    first_block = meta[0] * rows
    for side, ref in ((0, near), (1, far)):
        offset = meta[1] * half if side == 0 else (1 - meta[1]) * half

        def body(c, carry, side=side, ref=ref, offset=offset):
            copy(side, c).wait()
            row = c * chunk
            for i in range(0, chunk, 2):
                results = [
                    row_product([(ref, row + r, cols, offset + row + r)], panel, LAST)
                    for r in (i, i + 1)
                ]
                pair = join_pair(results[0], results[1], count)
                if side == 0:
                    keep_row[(row + i) // 2] = pair
                else:
                    send[send.shape[0] - 1, (row + i) // 2] = pair.astype(jnp.bfloat16)
                for r in (i, i + 1):
                    scatter_row(
                        panel[first_block + offset + row + r],
                        [(ref, row + r, cols, offset + row + r)],
                        total,
                    )
            return carry

        lax.fori_loop(0, chunks, body, 0)
    parts, pair_rows = sent.shape[0], sent.shape[1]
    for start, out, index in [
        (meta[1] * (blocks // 2) + p * 2 * pair_rows, sent, p) for p in range(parts)
    ] + [(first_block + meta[1] * half, mine, 0)]:

        def pack(i, carry, start=start, out=out, index=index):
            b = start + 2 * i
            out[index, i] = join_pair(
                panel[b].astype(jnp.float32), panel[b + 1].astype(jnp.float32), count
            ).astype(jnp.bfloat16)
            return carry

        lax.fori_loop(0, pair_rows, pack, 0, unroll=8 if pair_rows % 8 == 0 else 4)
    give_totals(count, rows, meta, keep, send, total)


def first_step(meta, cols, signs, stored, blocks):
    rows, slots, width = stored.shape[0], stored.shape[1], stored.shape[3]
    count = signs.shape[0] // blocks
    half = rows // 2
    chunk = min(16, half)
    parts = blocks // rows
    shape = jax.ShapeDtypeStruct
    piece = (half // 2, 2 * count, width)
    return pl.pallas_call(
        functools.partial(first_kernel, count, chunk, blocks),
        out_shape=(
            shape((blocks, PAD, width), jnp.bfloat16),
            shape((parts,) + piece, jnp.bfloat16),
            shape((1,) + piece, jnp.bfloat16),
            shape(piece, jnp.float32),
            shape((half, slots, width, width), jnp.bfloat16),
            shape((half, slots, width, width), jnp.bfloat16),
            shape((parts,) + piece, jnp.bfloat16),
            shape((parts + 1,) + piece, jnp.bfloat16),
        ),
        grid_spec=pltpu.PrefetchScalarGridSpec(
            num_scalar_prefetch=2,
            grid=(1,),
            in_specs=[in_hbm(), in_hbm()],
            out_specs=(whole(),) * 8,
            scratch_shapes=[
                pltpu.VMEM(signs.shape, jnp.int32),
                pltpu.VMEM((blocks, PAD, width), jnp.float32),
                pltpu.SemaphoreType.DMA(()),
                pltpu.SemaphoreType.DMA((2 * half // chunk,)),
            ],
        ),
        compiler_params=params(),
        cost_estimate=cost(2 * rows * slots, width),
        name="first_step",
    )(meta, cols, signs, stored)


def cost(stored, width):
    return pl.CostEstimate(
        flops=2 * stored * 128 * width * width,
        transcendentals=0,
        bytes_accessed=8 * stored * width * width,
    )


def forward_kernel(
    count, chunk, rows, inverse, where, meta, cols_own, cols_other, own, other, *rest
):
    panel, out = rest[-2:]
    unpack_into(panel, rest[: len(where)], where, count, meta)
    half = rows // 2
    block = meta[0] * rows + meta[1] * half

    def body(step, carry):
        row = step * chunk
        for i in range(0, chunk, 2):
            results = []
            for r in (i, i + 1):
                product = row_product(
                    [
                        (own, row + r, cols_own, meta[1] * half + row + r),
                        (other, row + r, cols_other, meta[1] * half + row + r),
                    ],
                    panel,
                    LAST,
                )
                results.append(panel[block + row + r].astype(jnp.float32) + inverse * product)
            out[0, (row + i) // 2] = join_pair(results[0], results[1], count).astype(
                jnp.bfloat16
            )
        return carry

    lax.fori_loop(0, half // chunk, body, 0)


def forward(meta, cols_own, cols_other, own, other, pieces, blocks, inverse, tokens):
    half, slots, width = own.shape[0], own.shape[1], own.shape[3]
    arrays = [array for array, _ in pieces]
    count = arrays[0].shape[2] // 2
    chunk = min(16, half)
    return pl.pallas_call(
        functools.partial(
            forward_kernel, count, chunk, 2 * half, inverse, [places for _, places in pieces]
        ),
        out_shape=(
            jax.ShapeDtypeStruct((blocks, PAD, width), jnp.bfloat16),
            jax.ShapeDtypeStruct((1, half // 2, 2 * count, width), jnp.bfloat16),
        ),
        grid_spec=pltpu.PrefetchScalarGridSpec(
            num_scalar_prefetch=3,
            grid=(1,),
            in_specs=[whole()] * (2 + len(arrays)) + [anywhere()] * len(tokens),
            out_specs=(whole(), whole()),
        ),
        compiler_params=params(),
        cost_estimate=cost(2 * half * slots, width),
        name="forward_step",
    )(meta, cols_own, cols_other, own, other, *arrays, *tokens)


def scatter_row(value, refs_and_rows, total):
    targets = []
    stored = []
    for ref, row, cols, col_row in refs_and_rows:
        for k in range(ref.shape[1]):
            targets.append(cols[k, col_row])
            stored.append(ref[row, k])
    terms = lax.dot_general(
        value, jnp.concatenate(stored, axis=1), FIRST, preferred_element_type=jnp.float32
    )
    width = stored[0].shape[1]
    for i, target in enumerate(targets):
        total[target] = total[target] + terms[:, i * width : (i + 1) * width]


def give_totals(count, rows, meta, keep, send, total):
    half = rows // 2
    pairs = half // 2
    for out, h in ((send, 1), (keep, 0)):
        for d in range(keep.shape[0]):
            base = (meta[0] ^ d) * rows + (meta[1] ^ h) * half

            def body(i, carry, out=out, base=base, d=d):
                out[d, i] = join_pair(
                    total[base + 2 * i], total[base + 2 * i + 1], count
                ).astype(jnp.bfloat16)
                return carry

            lax.fori_loop(0, pairs, body, 0, unroll=8 if pairs % 8 == 0 else 4)


def backward_kernel(
    count, chunk, meta, cols_own, cols_other, own, other, left, *rest
):
    keep, send, total = rest[-3:]
    half = own.shape[0]
    stored = ((own, cols_own), (other, cols_other))
    total[...] = jnp.zeros_like(total)

    def body(step, carry):
        for i in range(0, chunk, 2):
            pair = split_pair(left[0, (step * chunk + i) // 2], count)
            for r, value in zip((i, i + 1), pair):
                row = step * chunk + r
                scatter_row(
                    value.astype(jnp.bfloat16),
                    [(ref, row, cols, meta[1] * half + row) for ref, cols in stored],
                    total,
                )
        return carry

    lax.fori_loop(0, half // chunk, body, 0)
    give_totals(count, 2 * half, meta, keep, send, total)


def backward(meta, cols_own, cols_other, own, other, left, blocks, tokens):
    half, slots, width = own.shape[0], own.shape[1], own.shape[3]
    count = left.shape[2] // 2
    chunk = min(16, half)
    result = jax.ShapeDtypeStruct(
        (blocks // (2 * half), half // 2, 2 * count, width), jnp.bfloat16
    )
    return pl.pallas_call(
        functools.partial(backward_kernel, count, chunk),
        out_shape=(result, result),
        grid_spec=pltpu.PrefetchScalarGridSpec(
            num_scalar_prefetch=3,
            grid=(1,),
            in_specs=[whole()] * 3 + [anywhere()] * len(tokens),
            out_specs=(whole(), whole()),
            scratch_shapes=[pltpu.VMEM((blocks, PAD, width), jnp.float32)],
        ),
        compiler_params=params(),
        cost_estimate=cost(2 * half * slots, width),
        name="backward_step",
    )(meta, cols_own, cols_other, own, other, left, *tokens)


def gradient_kernel(scale, chunk, rows, terms, meta, cols, *refs):
    out = refs[-1]
    lefts = refs[: 4 * terms]
    rights = refs[4 * terms : 8 * terms]
    step = pl.program_id(0)
    slots = out.shape[1]
    contract = (((0,), (0,)), ((), ()))
    for r in range(chunk):
        row = step * chunk + r
        left = []
        for position, ref in enumerate(lefts):
            start = meta[0] * rows if position < terms else 0
            left.append(ref[start + row])
        left = jnp.concatenate(left, axis=0)
        right = []
        for k in range(slots):
            target = cols[k, row]
            right.append(jnp.concatenate([ref[target] for ref in rights], axis=0))
        product = lax.dot_general(
            left, jnp.concatenate(right, axis=1), contract, preferred_element_type=jnp.float32
        )
        width = out.shape[3]
        for k in range(slots):
            out[r, k] = (product[:, k * width : (k + 1) * width] * scale).astype(jnp.bfloat16)


def gradient(meta, cols, lefts, rights, rows, slots, scale):
    width = lefts[0].shape[2]
    chunk = min(16, rows)
    operands = list(lefts) + list(rights)
    return pl.pallas_call(
        functools.partial(gradient_kernel, scale, chunk, rows, len(lefts) // 4),
        out_shape=jax.ShapeDtypeStruct((rows, slots, width, width), jnp.bfloat16),
        grid_spec=pltpu.PrefetchScalarGridSpec(
            num_scalar_prefetch=2,
            grid=(rows // chunk,),
            in_specs=[whole()] * len(operands),
            out_specs=pl.BlockSpec((chunk, slots, width, width), lambda g, *_: (g, 0, 0, 0)),
        ),
        compiler_params=params(),
        name="gradient",
    )(meta, cols, *operands)


def tie(x, *tokens):
    return lax.optimization_barrier((x,) + tokens)[0]


def local(block_values, columns, probe_signs):
    rows, slots, width = block_values.shape[0], block_values.shape[1], block_values.shape[3]
    blocks, count = probe_signs.shape[0], probe_signs.shape[1]
    half = rows // 2
    n_var = lax.axis_size("var")
    n_probe = lax.axis_size("probe")
    groups = n_probe - 1
    inverse = 1.0 / math.sqrt(KS * width)
    meta = jnp.stack([lax.axis_index("var"), lax.axis_index("rep")]).astype(jnp.int32)
    signs = jnp.transpose(probe_signs, (1, 0, 2)).reshape(count * blocks, width)
    signs = pltpu.with_memory_space_constraint(signs, pltpu.HBM)
    block_values = pltpu.with_memory_space_constraint(block_values, pltpu.HBM)
    cols = columns.T

    def swap_rep(x):
        return lax.ppermute(x, "rep", [(0, 1), (1, 0)])

    def shift_var(x, bit):
        return lax.ppermute(x, "var", [(i, i ^ bit) for i in range(n_var)])

    def from_probes(x):
        return stack(
            [
                lax.ppermute(x, "probe", [(i, (i + d) % n_probe) for i in range(n_probe)])
                for d in range(1, n_probe)
            ]
        )

    def stack(arrays):
        return arrays[0] if len(arrays) == 1 else jnp.concatenate(arrays, axis=0)

    def wide(x):
        return x.astype(jnp.float32)

    def narrow(x):
        return x.astype(jnp.bfloat16)

    def home(d, h):
        return lambda v, r: (v ^ d) * rows + (r ^ h) * half

    def row_place(h):
        return lambda v, r: (r ^ h) * half

    def sign_place(p, h):
        return lambda v, r: (r ^ h) * (blocks // 2) + p * half

    def spot(label, h):
        if label == "row":
            return row_place(h)
        return home(label, h) if label < n_var else sign_place(label - n_var, h)

    def place(pieces, h):
        return [
            (array, [None if d is None else home(d, h) for d in ds]) for array, ds in pieces
        ]

    def jobs_of(entries):
        jobs = []
        for index in range(groups):
            for kind in ("blocks", "rows"):
                pieces = []
                for h in (0, 1):
                    for here, swapped, offset, labels in entries:
                        array, skip = (here, 0) if h == 0 else (swapped, offset)
                        where = [None] * array.shape[0]
                        for i, label in enumerate(labels):
                            if (label == "row") == (kind == "rows"):
                                where[skip + index * len(labels) + i] = spot(label, h)
                        if any(base is not None for base in where):
                            pieces.append((array, where))
                if pieces:
                    jobs.append((pieces, blocks if kind == "blocks" else rows))
        return jobs

    def swap_all(arrays, labels, extra, tokens):
        joined = list(arrays) + list(extra)
        if tokens:
            joined = [tie(array, *tokens) for array in joined]
        swapped = swap_rep(stack(joined))
        entries = []
        offset = 0
        for array, names in zip(arrays, labels):
            entries.append((array, swapped, offset, names))
            offset += array.shape[0]
        return swapped, entries, offset

    panel, sent, left_own, kept, near_blocks, far_blocks, keep, send = first_step(
        meta, cols, signs, block_values, blocks
    )
    received = swap_rep(send)
    updated = narrow(wide(left_own) + inverse * (kept + wide(received[n_var]))[None])
    other_blocks = swap_rep(tie(far_blocks, updated))
    other_columns = swap_rep(cols)
    right = [[panel]] + [[] for _ in range(groups)]
    left = [[panel]] + [[] for _ in range(groups)]
    sent = from_probes(tie(sent, updated))
    sign_labels = [n_var + p for p in range(n_var)]
    incoming, incoming_labels = [], []
    unpacked = []

    for step in range(3):
        parts = [wide(keep[d : d + 1]) + wide(received[d : d + 1]) for d in range(n_var)]
        if n_var == 4:
            far = shift_var(updated, 2)
            both = shift_var(stack([updated, narrow(parts[3])]), 1)
            near = both[:1]
            own_other = swap_rep(updated)
            crossed = shift_var(narrow(parts[2] + wide(both[1:])), 2)
            final = shift_var(stack([tie(far, own_other), narrow(parts[1])]), 1)
            last = final[:1]
            middle_other = swap_rep(stack([near, far]))
            summed = parts[0] + wide(final[1:]) + wide(crossed)
            held = [updated, near, far, last]
            others = [(own_other, [0]), (middle_other, [1, 2]), (swap_rep(last), [3])]
            window, settled = [both], [middle_other]
        else:
            bits = [1 << i for i in range(n_var.bit_length() - 1)]
            found = {0: updated}
            for bit in reversed(bits):
                for d in list(found):
                    found[d | bit] = shift_var(found[d], bit)
            held = [found[d] for d in range(n_var)]
            sums = dict(enumerate(parts))
            for bit in bits:
                for d in sorted(sums, reverse=True):
                    if d & bit:
                        sums[d ^ bit] = sums[d ^ bit] + wide(
                            shift_var(narrow(sums.pop(d)), bit)
                        )
            summed = sums[0]
            others = [(swap_rep(stack(held)), list(range(n_var)))]
            window, settled = [], []

        if step == 0:
            swapped, entries, _ = swap_all([sent], [sign_labels], [], window)
            jobs = jobs_of(entries)
        else:
            swapped, entries, offset = swap_all(incoming, incoming_labels, [left_own], window)
            tail = [None] * offset + [row_place(1)]
            jobs = jobs_of(entries)
            jobs.append(([(left_own, [row_place(0)]), (swapped, tail)], rows))
        found = list(unpack(meta, jobs))
        unpacked += found
        if step > 0:
            left[0].append(found.pop())
        for index in range(groups):
            right[1 + index].append(found.pop(0))
            left[1 + index].append(right[1 + index][0] if step == 0 else found.pop(0))

        left_own = narrow(wide(tie(left_own, swapped, *settled)) + inverse * summed)
        if step == 2 and n_var == 4:
            incoming = [from_probes(stack(held[:3])), from_probes(stack([last, left_own]))]
            incoming_labels = [[0, 1, 2], [3, "row"]]
        else:
            incoming = [from_probes(stack(held + [left_own]))]
            incoming_labels = [list(range(n_var)) + ["row"]]
        sources = place([(array, [d]) for d, array in enumerate(held)], 0) + place(others, 1)
        if step < 2:
            keep, send = backward(
                meta, cols, other_columns, near_blocks, other_blocks, left_own, blocks, []
            )
            received = swap_rep(send)
            panel, updated = forward(
                meta, cols, other_columns, near_blocks, other_blocks, sources, blocks, inverse,
                [send],
            )
            right[0].append(panel)

    jobs = [(sources, blocks)]
    jobs.append(([(left_own, [row_place(0)]), (swap_rep(left_own), [row_place(1)])], rows))
    ready = list(unpack(meta, jobs))
    right[0].append(ready[0])
    left[0].append(ready[1])
    entries = []
    for array, labels in zip(incoming, incoming_labels):
        tokens = ready + unpacked if array is incoming[-1] else []
        _, entry, _ = swap_all([array], [labels], [], tokens)
        entries += entry
    found = list(unpack(meta, jobs_of(entries)))
    for index in range(groups):
        right[1 + index].append(found.pop(0))
        left[1 + index].append(found.pop(0))

    lefts = [group[t] for t in range(4) for group in left]
    rights = [group[3 - t] for t in range(4) for group in right]
    scale = 1.0 / (count * n_probe)
    return gradient(meta, cols, lefts, rights, rows, slots, scale)


def solution(mesh):
    return jax.shard_map(
        local,
        mesh=mesh,
        in_specs=(
            P(("groups", "var"), "rep", None, None),
            P(("groups", "var"), "rep"),
            P("groups", "probe", None),
        ),
        out_specs=P(("groups", "var"), "rep", None, None),
        check_vma=False,
    )
```

```python
import functools
import math

import jax
import jax.numpy as jnp
from jax import lax
from jax.experimental import pallas as pl
from jax.experimental.pallas import tpu as pltpu
from jax.sharding import PartitionSpec as P

KS = 6
PAD = 16
VMEM_LIMIT = 16 * 1024 * 1024


def whole():
    return pl.BlockSpec(memory_space=pltpu.VMEM)


def params():
    return pltpu.CompilerParams(
        dimension_semantics=("arbitrary",), vmem_limit_bytes=VMEM_LIMIT
    )


def split_pair(pair, count):
    wide = pair.astype(jnp.float32)
    keep = lax.broadcasted_iota(jnp.int32, (PAD, wide.shape[1]), 0) < count
    first = jnp.where(keep, wide[:PAD], 0.0)
    second = jnp.where(keep, pltpu.roll(wide, count, 0)[:PAD], 0.0)
    return first, second


def join_pair(first, second, count):
    tail = jnp.zeros((2 * count - PAD, first.shape[1]), jnp.float32)
    low = jnp.concatenate([first, tail], axis=0)
    high = pltpu.roll(jnp.concatenate([second, tail], axis=0), count, 0)
    return low + high


def anywhere():
    return pl.BlockSpec(memory_space=pl.ANY)


def in_hbm():
    return pl.BlockSpec(memory_space=pltpu.HBM)


def unpack_into(panel, refs, where, count, meta):
    for ref, places in zip(refs, where):
        pairs = ref.shape[1]
        for index, base_of in enumerate(places):
            if base_of is None:
                continue
            base = base_of(meta[0], meta[1])

            def body(i, carry, ref=ref, base=base, index=index):
                first, second = split_pair(ref[index, i], count)
                panel[base + 2 * i] = first.astype(jnp.bfloat16)
                panel[base + 2 * i + 1] = second.astype(jnp.bfloat16)
                return carry

            lax.fori_loop(0, pairs, body, 0, unroll=8 if pairs % 8 == 0 else 4)


def unpack_kernel(count, wheres, skipped, meta, *refs):
    panels = refs[len(refs) - len(wheres) :]
    begin = 0
    for panel, where in zip(panels, wheres):
        unpack_into(panel, refs[begin : begin + len(where)], where, count, meta)
        begin += len(where)


def unpack(meta, jobs, tokens=()):
    arrays = [array for pieces, _ in jobs for array, _ in pieces]
    wheres = [[places for _, places in pieces] for pieces, _ in jobs]
    count = arrays[0].shape[2] // 2
    width = arrays[0].shape[3]
    return pl.pallas_call(
        functools.partial(unpack_kernel, count, wheres, len(tokens)),
        out_shape=[
            jax.ShapeDtypeStruct((blocks, PAD, width), jnp.bfloat16) for _, blocks in jobs
        ],
        grid_spec=pltpu.PrefetchScalarGridSpec(
            num_scalar_prefetch=1,
            grid=(1,),
            in_specs=[whole()] * len(arrays) + [anywhere()] * len(tokens),
            out_specs=[whole()] * len(jobs),
        ),
        compiler_params=params(),
        name="unpack_panels",
    )(meta, *arrays, *tokens)


def row_product(refs_and_rows, panel, contract):
    picked = []
    stored = []
    for ref, row, cols, col_row in refs_and_rows:
        for k in range(ref.shape[1]):
            picked.append(panel[cols[k, col_row]])
            stored.append(ref[row, k])
    return lax.dot_general(
        jnp.concatenate(picked, axis=1),
        jnp.concatenate(stored, axis=1),
        contract,
        preferred_element_type=jnp.float32,
    )


LAST = (((1,), (1,)), ((), ()))
FIRST = (((1,), (0,)), ((), ()))


def first_kernel(
    count, chunk, blocks, meta, cols, signs_hbm, stored,
    panel, sent, mine, keep_row, near, far, keep, send,
    signs, total, sign_sem, sems,
):
    half = near.shape[0]
    rows = 2 * half
    chunks = half // chunk
    rep = lax.axis_index("rep")

    def copy(side, c):
        place = (rep if side == 0 else 1 - rep) * half + c * chunk
        return pltpu.make_async_copy(
            stored.at[pl.ds(place, chunk)],
            (near, far)[side].at[pl.ds(c * chunk, chunk)],
            sems.at[side * chunks + c],
        )

    sign_copy = pltpu.make_async_copy(signs_hbm, signs, sign_sem)
    sign_copy.start()
    for side in (0, 1):
        for c in range(chunks):
            copy(side, c).start()
    total[...] = jnp.zeros_like(total)
    sign_copy.wait()
    pad = jnp.zeros((PAD - count, signs.shape[1]), jnp.float32)

    def convert(b, carry):
        value = signs[pl.ds(b, count, stride=blocks), :].astype(jnp.float32)
        panel[b] = jnp.concatenate([value, pad], axis=0).astype(jnp.bfloat16)
        return carry

    lax.fori_loop(0, blocks, convert, 0, unroll=8)
    first_block = meta[0] * rows
    for side, ref in ((0, near), (1, far)):
        offset = meta[1] * half if side == 0 else (1 - meta[1]) * half

        def body(c, carry, side=side, ref=ref, offset=offset):
            copy(side, c).wait()
            row = c * chunk
            for i in range(0, chunk, 2):
                results = [
                    row_product([(ref, row + r, cols, offset + row + r)], panel, LAST)
                    for r in (i, i + 1)
                ]
                pair = join_pair(results[0], results[1], count)
                if side == 0:
                    keep_row[(row + i) // 2] = pair
                else:
                    send[send.shape[0] - 1, (row + i) // 2] = pair.astype(jnp.bfloat16)
                for r in (i, i + 1):
                    scatter_row(
                        panel[first_block + offset + row + r],
                        [(ref, row + r, cols, offset + row + r)],
                        total,
                    )
            return carry

        lax.fori_loop(0, chunks, body, 0)
    parts, pair_rows = sent.shape[0], sent.shape[1]
    for start, out, index in [
        (meta[1] * (blocks // 2) + p * 2 * pair_rows, sent, p) for p in range(parts)
    ] + [(first_block + meta[1] * half, mine, 0)]:

        def pack(i, carry, start=start, out=out, index=index):
            b = start + 2 * i
            out[index, i] = join_pair(
                panel[b].astype(jnp.float32), panel[b + 1].astype(jnp.float32), count
            ).astype(jnp.bfloat16)
            return carry

        lax.fori_loop(0, pair_rows, pack, 0, unroll=8 if pair_rows % 8 == 0 else 4)
    give_totals(count, rows, meta, keep, send, total)


def first_step(meta, cols, signs, stored, blocks):
    rows, slots, width = stored.shape[0], stored.shape[1], stored.shape[3]
    count = signs.shape[0] // blocks
    half = rows // 2
    chunk = min(16, half)
    parts = blocks // rows
    shape = jax.ShapeDtypeStruct
    piece = (half // 2, 2 * count, width)
    return pl.pallas_call(
        functools.partial(first_kernel, count, chunk, blocks),
        out_shape=(
            shape((blocks, PAD, width), jnp.bfloat16),
            shape((parts,) + piece, jnp.bfloat16),
            shape((1,) + piece, jnp.bfloat16),
            shape(piece, jnp.float32),
            shape((half, slots, width, width), jnp.bfloat16),
            shape((half, slots, width, width), jnp.bfloat16),
            shape((parts,) + piece, jnp.bfloat16),
            shape((parts + 1,) + piece, jnp.bfloat16),
        ),
        grid_spec=pltpu.PrefetchScalarGridSpec(
            num_scalar_prefetch=2,
            grid=(1,),
            in_specs=[in_hbm(), in_hbm()],
            out_specs=(whole(),) * 8,
            scratch_shapes=[
                pltpu.VMEM(signs.shape, jnp.int32),
                pltpu.VMEM((blocks, PAD, width), jnp.float32),
                pltpu.SemaphoreType.DMA(()),
                pltpu.SemaphoreType.DMA((2 * half // chunk,)),
            ],
        ),
        compiler_params=params(),
        cost_estimate=cost(2 * rows * slots, width),
        name="first_step",
    )(meta, cols, signs, stored)


def cost(stored, width):
    return pl.CostEstimate(
        flops=2 * stored * 128 * width * width,
        transcendentals=0,
        bytes_accessed=8 * stored * width * width,
    )


def forward_kernel(
    count, chunk, rows, inverse, where, meta, cols_own, cols_other, own, other, *rest
):
    panel, out = rest[-2:]
    unpack_into(panel, rest[: len(where)], where, count, meta)
    half = rows // 2
    block = meta[0] * rows + meta[1] * half

    def body(step, carry):
        row = step * chunk
        for i in range(0, chunk, 2):
            results = []
            for r in (i, i + 1):
                product = row_product(
                    [
                        (own, row + r, cols_own, meta[1] * half + row + r),
                        (other, row + r, cols_other, meta[1] * half + row + r),
                    ],
                    panel,
                    LAST,
                )
                results.append(panel[block + row + r].astype(jnp.float32) + inverse * product)
            out[0, (row + i) // 2] = join_pair(results[0], results[1], count).astype(
                jnp.bfloat16
            )
        return carry

    lax.fori_loop(0, half // chunk, body, 0)


def forward(meta, cols_own, cols_other, own, other, pieces, blocks, inverse, tokens):
    half, slots, width = own.shape[0], own.shape[1], own.shape[3]
    arrays = [array for array, _ in pieces]
    count = arrays[0].shape[2] // 2
    chunk = min(16, half)
    return pl.pallas_call(
        functools.partial(
            forward_kernel, count, chunk, 2 * half, inverse, [places for _, places in pieces]
        ),
        out_shape=(
            jax.ShapeDtypeStruct((blocks, PAD, width), jnp.bfloat16),
            jax.ShapeDtypeStruct((1, half // 2, 2 * count, width), jnp.bfloat16),
        ),
        grid_spec=pltpu.PrefetchScalarGridSpec(
            num_scalar_prefetch=3,
            grid=(1,),
            in_specs=[whole()] * (2 + len(arrays)) + [anywhere()] * len(tokens),
            out_specs=(whole(), whole()),
        ),
        compiler_params=params(),
        cost_estimate=cost(2 * half * slots, width),
        name="forward_step",
    )(meta, cols_own, cols_other, own, other, *arrays, *tokens)


def scatter_row(value, refs_and_rows, total):
    targets = []
    stored = []
    for ref, row, cols, col_row in refs_and_rows:
        for k in range(ref.shape[1]):
            targets.append(cols[k, col_row])
            stored.append(ref[row, k])
    terms = lax.dot_general(
        value, jnp.concatenate(stored, axis=1), FIRST, preferred_element_type=jnp.float32
    )
    width = stored[0].shape[1]
    for i, target in enumerate(targets):
        total[target] = total[target] + terms[:, i * width : (i + 1) * width]


def give_totals(count, rows, meta, keep, send, total):
    half = rows // 2
    pairs = half // 2
    for out, h in ((send, 1), (keep, 0)):
        for d in range(keep.shape[0]):
            base = (meta[0] ^ d) * rows + (meta[1] ^ h) * half

            def body(i, carry, out=out, base=base, d=d):
                out[d, i] = join_pair(
                    total[base + 2 * i], total[base + 2 * i + 1], count
                ).astype(jnp.bfloat16)
                return carry

            lax.fori_loop(0, pairs, body, 0, unroll=8 if pairs % 8 == 0 else 4)


def backward_kernel(
    count, chunk, meta, cols_own, cols_other, own, other, left, *rest
):
    keep, send, total = rest[-3:]
    half = own.shape[0]
    stored = ((own, cols_own), (other, cols_other))
    total[...] = jnp.zeros_like(total)

    def body(step, carry):
        for i in range(0, chunk, 2):
            pair = split_pair(left[0, (step * chunk + i) // 2], count)
            for r, value in zip((i, i + 1), pair):
                row = step * chunk + r
                scatter_row(
                    value.astype(jnp.bfloat16),
                    [(ref, row, cols, meta[1] * half + row) for ref, cols in stored],
                    total,
                )
        return carry

    lax.fori_loop(0, half // chunk, body, 0)
    give_totals(count, 2 * half, meta, keep, send, total)


def backward(meta, cols_own, cols_other, own, other, left, blocks, tokens):
    half, slots, width = own.shape[0], own.shape[1], own.shape[3]
    count = left.shape[2] // 2
    chunk = min(16, half)
    result = jax.ShapeDtypeStruct(
        (blocks // (2 * half), half // 2, 2 * count, width), jnp.bfloat16
    )
    return pl.pallas_call(
        functools.partial(backward_kernel, count, chunk),
        out_shape=(result, result),
        grid_spec=pltpu.PrefetchScalarGridSpec(
            num_scalar_prefetch=3,
            grid=(1,),
            in_specs=[whole()] * 3 + [anywhere()] * len(tokens),
            out_specs=(whole(), whole()),
            scratch_shapes=[pltpu.VMEM((blocks, PAD, width), jnp.float32)],
        ),
        compiler_params=params(),
        cost_estimate=cost(2 * half * slots, width),
        name="backward_step",
    )(meta, cols_own, cols_other, own, other, left, *tokens)


def gradient_kernel(scale, chunk, rows, terms, meta, cols, *refs):
    out = refs[-1]
    lefts = refs[: 4 * terms]
    rights = refs[4 * terms : 8 * terms]
    step = pl.program_id(0)
    slots = out.shape[1]
    contract = (((0,), (0,)), ((), ()))
    for r in range(chunk):
        row = step * chunk + r
        left = []
        for position, ref in enumerate(lefts):
            start = meta[0] * rows if position < terms else 0
            left.append(ref[start + row])
        left = jnp.concatenate(left, axis=0)
        right = []
        for k in range(slots):
            target = cols[k, row]
            right.append(jnp.concatenate([ref[target] for ref in rights], axis=0))
        product = lax.dot_general(
            left, jnp.concatenate(right, axis=1), contract, preferred_element_type=jnp.float32
        )
        width = out.shape[3]
        for k in range(slots):
            out[r, k] = (product[:, k * width : (k + 1) * width] * scale).astype(jnp.bfloat16)


def gradient(meta, cols, lefts, rights, rows, slots, scale):
    width = lefts[0].shape[2]
    chunk = min(16, rows)
    operands = list(lefts) + list(rights)
    return pl.pallas_call(
        functools.partial(gradient_kernel, scale, chunk, rows, len(lefts) // 4),
        out_shape=jax.ShapeDtypeStruct((rows, slots, width, width), jnp.bfloat16),
        grid_spec=pltpu.PrefetchScalarGridSpec(
            num_scalar_prefetch=2,
            grid=(rows // chunk,),
            in_specs=[whole()] * len(operands),
            out_specs=pl.BlockSpec((chunk, slots, width, width), lambda g, *_: (g, 0, 0, 0)),
        ),
        compiler_params=params(),
        name="gradient",
    )(meta, cols, *operands)


def tie(x, *tokens):
    return lax.optimization_barrier((x,) + tokens)[0]


def local(block_values, columns, probe_signs):
    rows, slots, width = block_values.shape[0], block_values.shape[1], block_values.shape[3]
    blocks, count = probe_signs.shape[0], probe_signs.shape[1]
    half = rows // 2
    n_var = lax.axis_size("var")
    n_probe = lax.axis_size("probe")
    groups = n_probe - 1
    inverse = 1.0 / math.sqrt(KS * width)
    meta = jnp.stack([lax.axis_index("var"), lax.axis_index("rep")]).astype(jnp.int32)
    signs = jnp.transpose(probe_signs, (1, 0, 2)).reshape(count * blocks, width)
    signs = pltpu.with_memory_space_constraint(signs, pltpu.HBM)
    block_values = pltpu.with_memory_space_constraint(block_values, pltpu.HBM)
    cols = columns.T
    cols_hbm = pltpu.with_memory_space_constraint(cols, pltpu.HBM)

    def swap_rep(x):
        return lax.ppermute(x, "rep", [(0, 1), (1, 0)])

    def shift_var(x, bit):
        return lax.ppermute(x, "var", [(i, i ^ bit) for i in range(n_var)])

    def from_probes(x):
        return stack(
            [
                lax.ppermute(x, "probe", [(i, (i + d) % n_probe) for i in range(n_probe)])
                for d in range(1, n_probe)
            ]
        )

    def stack(arrays):
        return arrays[0] if len(arrays) == 1 else jnp.concatenate(arrays, axis=0)

    def wide(x):
        return x.astype(jnp.float32)

    def narrow(x):
        return x.astype(jnp.bfloat16)

    def home(d, h):
        return lambda v, r: (v ^ d) * rows + (r ^ h) * half

    def row_place(h):
        return lambda v, r: (r ^ h) * half

    def sign_place(p, h):
        return lambda v, r: (r ^ h) * (blocks // 2) + p * half

    def spot(label, h):
        if label == "row":
            return row_place(h)
        return home(label, h) if label < n_var else sign_place(label - n_var, h)

    def place(pieces, h):
        return [
            (array, [None if d is None else home(d, h) for d in ds]) for array, ds in pieces
        ]

    def jobs_of(entries):
        jobs = []
        for index in range(groups):
            for kind in ("blocks", "rows"):
                pieces = []
                for h in (0, 1):
                    for here, swapped, offset, labels in entries:
                        array, skip = (here, 0) if h == 0 else (swapped, offset)
                        where = [None] * array.shape[0]
                        for i, label in enumerate(labels):
                            if (label == "row") == (kind == "rows"):
                                where[skip + index * len(labels) + i] = spot(label, h)
                        if any(base is not None for base in where):
                            pieces.append((array, where))
                if pieces:
                    jobs.append((pieces, blocks if kind == "blocks" else rows))
        return jobs

    def swap_all(arrays, labels, extra, tokens):
        joined = list(arrays) + list(extra)
        if tokens:
            joined = [tie(array, *tokens) for array in joined]
        swapped = swap_rep(stack(joined))
        entries = []
        offset = 0
        for array, names in zip(arrays, labels):
            entries.append((array, swapped, offset, names))
            offset += array.shape[0]
        return swapped, entries, offset

    panel, sent, left_own, kept, near_blocks, far_blocks, keep, send = first_step(
        meta, cols_hbm, signs, block_values, blocks
    )
    received = swap_rep(send)
    updated = narrow(wide(left_own) + inverse * (kept + wide(received[n_var]))[None])
    other_blocks = swap_rep(tie(far_blocks, updated))
    other_columns = swap_rep(cols)
    right = [[panel]] + [[] for _ in range(groups)]
    left = [[panel]] + [[] for _ in range(groups)]
    sent = from_probes(tie(sent, updated))
    sign_labels = [n_var + p for p in range(n_var)]
    incoming, incoming_labels = [], []
    unpacked = []

    for step in range(3):
        parts = [wide(keep[d : d + 1]) + wide(received[d : d + 1]) for d in range(n_var)]
        if n_var == 4:
            far = shift_var(updated, 2)
            both = shift_var(stack([updated, narrow(parts[3])]), 1)
            near = both[:1]
            own_other = swap_rep(updated)
            crossed = shift_var(narrow(parts[2] + wide(both[1:])), 2)
            final = shift_var(stack([tie(far, own_other), narrow(parts[1])]), 1)
            last = final[:1]
            middle_other = swap_rep(stack([near, far]))
            summed = parts[0] + wide(final[1:]) + wide(crossed)
            held = [updated, near, far, last]
            others = [(own_other, [0]), (middle_other, [1, 2]), (swap_rep(last), [3])]
            window, settled = [both], [middle_other] if step > 0 else []
        else:
            bits = [1 << i for i in range(n_var.bit_length() - 1)]
            found = {0: updated}
            for bit in reversed(bits):
                for d in list(found):
                    found[d | bit] = shift_var(found[d], bit)
            held = [found[d] for d in range(n_var)]
            sums = dict(enumerate(parts))
            for bit in bits:
                for d in sorted(sums, reverse=True):
                    if d & bit:
                        sums[d ^ bit] = sums[d ^ bit] + wide(
                            shift_var(narrow(sums.pop(d)), bit)
                        )
            summed = sums[0]
            others = [(swap_rep(stack(held)), list(range(n_var)))]
            window, settled = [], []

        if step == 0:
            swapped, entries, _ = swap_all([sent], [sign_labels], [], window)
            jobs = jobs_of(entries)
        else:
            swapped, entries, offset = swap_all(incoming, incoming_labels, [left_own], window)
            tail = [None] * offset + [row_place(1)]
            jobs = jobs_of(entries)
            jobs.append(([(left_own, [row_place(0)]), (swapped, tail)], rows))
        found = list(unpack(meta, jobs))
        unpacked += found
        if step > 0:
            left[0].append(found.pop())
        for index in range(groups):
            right[1 + index].append(found.pop(0))
            left[1 + index].append(right[1 + index][0] if step == 0 else found.pop(0))

        left_own = narrow(wide(tie(left_own, swapped, *settled)) + inverse * summed)
        if step == 2 and n_var == 4:
            incoming = [from_probes(stack(held[:3])), from_probes(stack([last, left_own]))]
            incoming_labels = [[0, 1, 2], [3, "row"]]
        else:
            incoming = [from_probes(stack(held + [left_own]))]
            incoming_labels = [list(range(n_var)) + ["row"]]
        sources = place([(array, [d]) for d, array in enumerate(held)], 0) + place(others, 1)
        if step < 2:
            keep, send = backward(
                meta, cols, other_columns, near_blocks, other_blocks, left_own, blocks, []
            )
            received = swap_rep(send)
            panel, updated = forward(
                meta, cols, other_columns, near_blocks, other_blocks, sources, blocks, inverse,
                [send],
            )
            right[0].append(panel)

    jobs = [(sources, blocks)]
    jobs.append(([(left_own, [row_place(0)]), (swap_rep(left_own), [row_place(1)])], rows))
    ready = list(unpack(meta, jobs))
    right[0].append(ready[0])
    left[0].append(ready[1])
    entries = []
    for array, labels in zip(incoming, incoming_labels):
        tokens = ready + unpacked if array is incoming[-1] else []
        _, entry, _ = swap_all([array], [labels], [], tokens)
        entries += entry
    found = list(unpack(meta, jobs_of(entries)))
    for index in range(groups):
        right[1 + index].append(found.pop(0))
        left[1 + index].append(found.pop(0))

    lefts = [group[t] for t in range(4) for group in left]
    rights = [group[3 - t] for t in range(4) for group in right]
    scale = 1.0 / (count * n_probe)
    return gradient(meta, cols, lefts, rights, rows, slots, scale)


def solution(mesh):
    return jax.shard_map(
        local,
        mesh=mesh,
        in_specs=(
            P(("groups", "var"), "rep", None, None),
            P(("groups", "var"), "rep"),
            P("groups", "probe", None),
        ),
        out_specs=P(("groups", "var"), "rep", None, None),
        check_vma=False,
    )
```

```python
import functools
import math

import jax
import jax.numpy as jnp
from jax import lax
from jax.experimental import pallas as pl
from jax.experimental.pallas import tpu as pltpu
from jax.sharding import PartitionSpec as P

KS = 6
PAD = 16
GRADIENT_ROWS = 8
VMEM_LIMIT = 16 * 1024 * 1024


def whole():
    return pl.BlockSpec(memory_space=pltpu.VMEM)


def params():
    return pltpu.CompilerParams(
        dimension_semantics=("arbitrary",), vmem_limit_bytes=VMEM_LIMIT
    )


def split_pair(pair, count):
    wide = pair.astype(jnp.float32)
    keep = lax.broadcasted_iota(jnp.int32, (PAD, wide.shape[1]), 0) < count
    first = jnp.where(keep, wide[:PAD], 0.0)
    second = jnp.where(keep, pltpu.roll(wide, count, 0)[:PAD], 0.0)
    return first, second


def join_pair(first, second, count):
    tail = jnp.zeros((2 * count - PAD, first.shape[1]), jnp.float32)
    low = jnp.concatenate([first, tail], axis=0)
    high = pltpu.roll(jnp.concatenate([second, tail], axis=0), count, 0)
    return low + high


def anywhere():
    return pl.BlockSpec(memory_space=pl.ANY)


def in_hbm():
    return pl.BlockSpec(memory_space=pltpu.HBM)


def unpack_into(panel, refs, where, count, meta):
    for ref, places in zip(refs, where):
        pairs = ref.shape[1]
        for index, base_of in enumerate(places):
            if base_of is None:
                continue
            base = base_of(meta[0], meta[1])

            def body(i, carry, ref=ref, base=base, index=index):
                first, second = split_pair(ref[index, i], count)
                panel[base + 2 * i] = first.astype(jnp.bfloat16)
                panel[base + 2 * i + 1] = second.astype(jnp.bfloat16)
                return carry

            lax.fori_loop(0, pairs, body, 0, unroll=8 if pairs % 8 == 0 else 4)


def unpack_kernel(count, wheres, skipped, meta, *refs):
    panels = refs[len(refs) - len(wheres) :]
    begin = 0
    for panel, where in zip(panels, wheres):
        unpack_into(panel, refs[begin : begin + len(where)], where, count, meta)
        begin += len(where)


def unpack(meta, jobs, tokens=()):
    arrays = [array for pieces, _ in jobs for array, _ in pieces]
    wheres = [[places for _, places in pieces] for pieces, _ in jobs]
    count = arrays[0].shape[2] // 2
    width = arrays[0].shape[3]
    return pl.pallas_call(
        functools.partial(unpack_kernel, count, wheres, len(tokens)),
        out_shape=[
            jax.ShapeDtypeStruct((blocks, PAD, width), jnp.bfloat16) for _, blocks in jobs
        ],
        grid_spec=pltpu.PrefetchScalarGridSpec(
            num_scalar_prefetch=1,
            grid=(1,),
            in_specs=[whole()] * len(arrays) + [anywhere()] * len(tokens),
            out_specs=[whole()] * len(jobs),
        ),
        compiler_params=params(),
        name="unpack_panels",
    )(meta, *arrays, *tokens)


def row_product(refs_and_rows, panel, contract):
    picked = []
    stored = []
    for ref, row, cols, col_row in refs_and_rows:
        for k in range(ref.shape[1]):
            picked.append(panel[cols[k, col_row]])
            stored.append(ref[row, k])
    return lax.dot_general(
        jnp.concatenate(picked, axis=1),
        jnp.concatenate(stored, axis=1),
        contract,
        preferred_element_type=jnp.float32,
    )


LAST = (((1,), (1,)), ((), ()))
FIRST = (((1,), (0,)), ((), ()))


def first_kernel(
    count, chunk, blocks, meta, cols, signs_hbm, stored,
    panel, sent, mine, keep_row, near, far, keep, send,
    signs, total, sign_sem, sems,
):
    half = near.shape[0]
    rows = 2 * half
    chunks = half // chunk
    rep = lax.axis_index("rep")

    def copy(side, c):
        place = (rep if side == 0 else 1 - rep) * half + c * chunk
        return pltpu.make_async_copy(
            stored.at[pl.ds(place, chunk)],
            (near, far)[side].at[pl.ds(c * chunk, chunk)],
            sems.at[side * chunks + c],
        )

    sign_copy = pltpu.make_async_copy(signs_hbm, signs, sign_sem)
    sign_copy.start()
    for side in (0, 1):
        for c in range(chunks):
            copy(side, c).start()
    total[...] = jnp.zeros_like(total)
    sign_copy.wait()
    pad = jnp.zeros((PAD - count, signs.shape[1]), jnp.float32)

    def convert(b, carry):
        value = signs[pl.ds(b, count, stride=blocks), :].astype(jnp.float32)
        panel[b] = jnp.concatenate([value, pad], axis=0).astype(jnp.bfloat16)
        return carry

    lax.fori_loop(0, blocks, convert, 0, unroll=8)
    first_block = meta[0] * rows
    for side, ref in ((0, near), (1, far)):
        offset = meta[1] * half if side == 0 else (1 - meta[1]) * half

        def body(c, carry, side=side, ref=ref, offset=offset):
            copy(side, c).wait()
            row = c * chunk
            for i in range(0, chunk, 2):
                results = [
                    row_product([(ref, row + r, cols, offset + row + r)], panel, LAST)
                    for r in (i, i + 1)
                ]
                pair = join_pair(results[0], results[1], count)
                if side == 0:
                    keep_row[(row + i) // 2] = pair
                else:
                    send[send.shape[0] - 1, (row + i) // 2] = pair.astype(jnp.bfloat16)
                for r in (i, i + 1):
                    scatter_row(
                        panel[first_block + offset + row + r],
                        [(ref, row + r, cols, offset + row + r)],
                        total,
                    )
            return carry

        lax.fori_loop(0, chunks, body, 0)
    parts, pair_rows = sent.shape[0], sent.shape[1]
    for start, out, index in [
        (meta[1] * (blocks // 2) + p * 2 * pair_rows, sent, p) for p in range(parts)
    ] + [(first_block + meta[1] * half, mine, 0)]:

        def pack(i, carry, start=start, out=out, index=index):
            b = start + 2 * i
            out[index, i] = join_pair(
                panel[b].astype(jnp.float32), panel[b + 1].astype(jnp.float32), count
            ).astype(jnp.bfloat16)
            return carry

        lax.fori_loop(0, pair_rows, pack, 0, unroll=8 if pair_rows % 8 == 0 else 4)
    give_totals(count, rows, meta, keep, send, total)


def first_step(meta, cols, signs, stored, blocks):
    rows, slots, width = stored.shape[0], stored.shape[1], stored.shape[3]
    count = signs.shape[0] // blocks
    half = rows // 2
    chunk = min(32, half)
    parts = blocks // rows
    shape = jax.ShapeDtypeStruct
    piece = (half // 2, 2 * count, width)
    return pl.pallas_call(
        functools.partial(first_kernel, count, chunk, blocks),
        out_shape=(
            shape((blocks, PAD, width), jnp.bfloat16),
            shape((parts,) + piece, jnp.bfloat16),
            shape((1,) + piece, jnp.bfloat16),
            shape(piece, jnp.float32),
            shape((half, slots, width, width), jnp.bfloat16),
            shape((half, slots, width, width), jnp.bfloat16),
            shape((parts,) + piece, jnp.bfloat16),
            shape((parts + 1,) + piece, jnp.bfloat16),
        ),
        grid_spec=pltpu.PrefetchScalarGridSpec(
            num_scalar_prefetch=2,
            grid=(1,),
            in_specs=[in_hbm(), in_hbm()],
            out_specs=(whole(),) * 8,
            scratch_shapes=[
                pltpu.VMEM(signs.shape, jnp.int32),
                pltpu.VMEM((blocks, PAD, width), jnp.float32),
                pltpu.SemaphoreType.DMA(()),
                pltpu.SemaphoreType.DMA((2 * half // chunk,)),
            ],
        ),
        compiler_params=params(),
        cost_estimate=cost(2 * rows * slots, width),
        name="first_step",
    )(meta, cols, signs, stored)


def cost(stored, width):
    return pl.CostEstimate(
        flops=2 * stored * 128 * width * width,
        transcendentals=0,
        bytes_accessed=8 * stored * width * width,
    )


def forward_kernel(
    count, chunk, rows, inverse, where, meta, cols_own, cols_other, own, other, *rest
):
    panel, out = rest[-2:]
    unpack_into(panel, rest[: len(where)], where, count, meta)
    half = rows // 2
    block = meta[0] * rows + meta[1] * half

    def body(step, carry):
        row = step * chunk
        for i in range(0, chunk, 2):
            results = []
            for r in (i, i + 1):
                product = row_product(
                    [
                        (own, row + r, cols_own, meta[1] * half + row + r),
                        (other, row + r, cols_other, meta[1] * half + row + r),
                    ],
                    panel,
                    LAST,
                )
                results.append(panel[block + row + r].astype(jnp.float32) + inverse * product)
            out[0, (row + i) // 2] = join_pair(results[0], results[1], count).astype(
                jnp.bfloat16
            )
        return carry

    lax.fori_loop(0, half // chunk, body, 0)


def forward(meta, cols_own, cols_other, own, other, pieces, blocks, inverse, tokens):
    half, slots, width = own.shape[0], own.shape[1], own.shape[3]
    arrays = [array for array, _ in pieces]
    count = arrays[0].shape[2] // 2
    chunk = min(32, half)
    return pl.pallas_call(
        functools.partial(
            forward_kernel, count, chunk, 2 * half, inverse, [places for _, places in pieces]
        ),
        out_shape=(
            jax.ShapeDtypeStruct((blocks, PAD, width), jnp.bfloat16),
            jax.ShapeDtypeStruct((1, half // 2, 2 * count, width), jnp.bfloat16),
        ),
        grid_spec=pltpu.PrefetchScalarGridSpec(
            num_scalar_prefetch=3,
            grid=(1,),
            in_specs=[whole()] * (2 + len(arrays)) + [anywhere()] * len(tokens),
            out_specs=(whole(), whole()),
        ),
        compiler_params=params(),
        cost_estimate=cost(2 * half * slots, width),
        name="forward_step",
    )(meta, cols_own, cols_other, own, other, *arrays, *tokens)


def scatter_row(value, refs_and_rows, total):
    targets = []
    stored = []
    for ref, row, cols, col_row in refs_and_rows:
        for k in range(ref.shape[1]):
            targets.append(cols[k, col_row])
            stored.append(ref[row, k])
    terms = lax.dot_general(
        value, jnp.concatenate(stored, axis=1), FIRST, preferred_element_type=jnp.float32
    )
    width = stored[0].shape[1]
    for i, target in enumerate(targets):
        total[target] = total[target] + terms[:, i * width : (i + 1) * width]


def give_totals(count, rows, meta, keep, send, total):
    half = rows // 2
    pairs = half // 2
    for out, h in ((send, 1), (keep, 0)):
        for d in range(keep.shape[0]):
            base = (meta[0] ^ d) * rows + (meta[1] ^ h) * half

            def body(i, carry, out=out, base=base, d=d):
                out[d, i] = join_pair(
                    total[base + 2 * i], total[base + 2 * i + 1], count
                ).astype(jnp.bfloat16)
                return carry

            lax.fori_loop(0, pairs, body, 0, unroll=8 if pairs % 8 == 0 else 4)


def backward_kernel(
    count, chunk, meta, cols_own, cols_other, own, other, left, *rest
):
    keep, send, total = rest[-3:]
    half = own.shape[0]
    stored = ((own, cols_own), (other, cols_other))
    total[...] = jnp.zeros_like(total)

    def body(step, carry):
        for i in range(0, chunk, 2):
            pair = split_pair(left[0, (step * chunk + i) // 2], count)
            for r, value in zip((i, i + 1), pair):
                row = step * chunk + r
                scatter_row(
                    value.astype(jnp.bfloat16),
                    [(ref, row, cols, meta[1] * half + row) for ref, cols in stored],
                    total,
                )
        return carry

    lax.fori_loop(0, half // chunk, body, 0)
    give_totals(count, 2 * half, meta, keep, send, total)


def backward(meta, cols_own, cols_other, own, other, left, blocks, tokens):
    half, slots, width = own.shape[0], own.shape[1], own.shape[3]
    count = left.shape[2] // 2
    chunk = min(32, half)
    result = jax.ShapeDtypeStruct(
        (blocks // (2 * half), half // 2, 2 * count, width), jnp.bfloat16
    )
    return pl.pallas_call(
        functools.partial(backward_kernel, count, chunk),
        out_shape=(result, result),
        grid_spec=pltpu.PrefetchScalarGridSpec(
            num_scalar_prefetch=3,
            grid=(1,),
            in_specs=[whole()] * 3 + [anywhere()] * len(tokens),
            out_specs=(whole(), whole()),
            scratch_shapes=[pltpu.VMEM((blocks, PAD, width), jnp.float32)],
        ),
        compiler_params=params(),
        cost_estimate=cost(2 * half * slots, width),
        name="backward_step",
    )(meta, cols_own, cols_other, own, other, left, *tokens)


def gradient_kernel(scale, chunk, rows, terms, meta, cols, *refs):
    out, made, sems = refs[-3:]
    lefts = refs[: 4 * terms]
    rights = refs[4 * terms : 8 * terms]
    slots, width = out.shape[1], out.shape[3]
    contract = (((0,), (0,)), ((), ()))

    def copy(step):
        part = pl.ds(step * chunk, chunk)
        return pltpu.make_async_copy(made.at[part], out.at[part], sems.at[step])

    def body(step, carry):
        for r in range(chunk):
            row = step * chunk + r
            left = []
            for position, ref in enumerate(lefts):
                start = meta[0] * rows if position < terms else 0
                left.append(ref[start + row])
            left = jnp.concatenate(left, axis=0)
            right = []
            for k in range(slots):
                target = cols[k, row]
                right.append(jnp.concatenate([ref[target] for ref in rights], axis=0))
            product = lax.dot_general(
                left, jnp.concatenate(right, axis=1), contract, preferred_element_type=jnp.float32
            )
            for k in range(slots):
                made[row, k] = (product[:, k * width : (k + 1) * width] * scale).astype(
                    jnp.bfloat16
                )
        copy(step).start()
        return carry

    for step in range(rows // chunk):
        body(step, 0)
    for step in range(rows // chunk):
        copy(step).wait()


def gradient(meta, cols, lefts, rights, rows, slots, scale):
    width = lefts[0].shape[2]
    chunk = min(GRADIENT_ROWS, rows)
    operands = list(lefts) + list(rights)
    shape = (rows, slots, width, width)
    return pl.pallas_call(
        functools.partial(gradient_kernel, scale, chunk, rows, len(lefts) // 4),
        out_shape=jax.ShapeDtypeStruct(shape, jnp.bfloat16),
        grid_spec=pltpu.PrefetchScalarGridSpec(
            num_scalar_prefetch=2,
            grid=(1,),
            in_specs=[whole()] * len(operands),
            out_specs=anywhere(),
            scratch_shapes=[
                pltpu.VMEM(shape, jnp.bfloat16),
                pltpu.SemaphoreType.DMA((rows // chunk,)),
            ],
        ),
        compiler_params=params(),
        name="gradient",
    )(meta, cols, *operands)


def tie(x, *tokens):
    return lax.optimization_barrier((x,) + tokens)[0]


def local(block_values, columns, probe_signs):
    rows, slots, width = block_values.shape[0], block_values.shape[1], block_values.shape[3]
    blocks, count = probe_signs.shape[0], probe_signs.shape[1]
    half = rows // 2
    n_var = lax.axis_size("var")
    n_probe = lax.axis_size("probe")
    groups = n_probe - 1
    inverse = 1.0 / math.sqrt(KS * width)
    meta = jnp.stack([lax.axis_index("var"), lax.axis_index("rep")]).astype(jnp.int32)
    signs = jnp.transpose(probe_signs, (1, 0, 2)).reshape(count * blocks, width)
    signs = pltpu.with_memory_space_constraint(signs, pltpu.HBM)
    block_values = pltpu.with_memory_space_constraint(block_values, pltpu.HBM)
    cols = columns.T
    cols_hbm = pltpu.with_memory_space_constraint(cols, pltpu.HBM)

    def swap_rep(x):
        return lax.ppermute(x, "rep", [(0, 1), (1, 0)])

    def shift_var(x, bit):
        return lax.ppermute(x, "var", [(i, i ^ bit) for i in range(n_var)])

    def from_probes(x):
        return stack(
            [
                lax.ppermute(x, "probe", [(i, (i + d) % n_probe) for i in range(n_probe)])
                for d in range(1, n_probe)
            ]
        )

    def stack(arrays):
        return arrays[0] if len(arrays) == 1 else jnp.concatenate(arrays, axis=0)

    def wide(x):
        return x.astype(jnp.float32)

    def narrow(x):
        return x.astype(jnp.bfloat16)

    def home(d, h):
        return lambda v, r: (v ^ d) * rows + (r ^ h) * half

    def row_place(h):
        return lambda v, r: (r ^ h) * half

    def sign_place(p, h):
        return lambda v, r: (r ^ h) * (blocks // 2) + p * half

    def spot(label, h):
        if label == "row":
            return row_place(h)
        return home(label, h) if label < n_var else sign_place(label - n_var, h)

    def place(pieces, h):
        return [
            (array, [None if d is None else home(d, h) for d in ds]) for array, ds in pieces
        ]

    def jobs_of(entries):
        jobs = []
        for index in range(groups):
            for kind in ("blocks", "rows"):
                pieces = []
                for h in (0, 1):
                    for here, swapped, offset, labels in entries:
                        array, skip = (here, 0) if h == 0 else (swapped, offset)
                        where = [None] * array.shape[0]
                        for i, label in enumerate(labels):
                            if (label == "row") == (kind == "rows"):
                                where[skip + index * len(labels) + i] = spot(label, h)
                        if any(base is not None for base in where):
                            pieces.append((array, where))
                if pieces:
                    jobs.append((pieces, blocks if kind == "blocks" else rows))
        return jobs

    def swap_all(arrays, labels, extra, tokens):
        joined = list(arrays) + list(extra)
        if tokens:
            joined = [tie(array, *tokens) for array in joined]
        swapped = swap_rep(stack(joined))
        entries = []
        offset = 0
        for array, names in zip(arrays, labels):
            entries.append((array, swapped, offset, names))
            offset += array.shape[0]
        return swapped, entries, offset

    panel, sent, left_own, kept, near_blocks, far_blocks, keep, send = first_step(
        meta, cols_hbm, signs, block_values, blocks
    )
    received = swap_rep(send)
    updated = narrow(wide(left_own) + inverse * (kept + wide(received[n_var]))[None])
    other_blocks = swap_rep(tie(far_blocks, updated))
    other_columns = swap_rep(cols)
    right = [[panel]] + [[] for _ in range(groups)]
    left = [[panel]] + [[] for _ in range(groups)]
    sent = from_probes(tie(sent, updated))
    sign_labels = [n_var + p for p in range(n_var)]
    incoming, incoming_labels = [], []
    unpacked = []

    for step in range(3):
        parts = [wide(keep[d : d + 1]) + wide(received[d : d + 1]) for d in range(n_var)]
        if n_var == 4:
            far = shift_var(updated, 2)
            both = shift_var(stack([updated, narrow(parts[3])]), 1)
            near = both[:1]
            own_other = swap_rep(updated)
            crossed = shift_var(narrow(parts[2] + wide(both[1:])), 2)
            final = shift_var(stack([tie(far, own_other), narrow(parts[1])]), 1)
            last = final[:1]
            middle_other = swap_rep(stack([near, far]))
            summed = parts[0] + wide(final[1:]) + wide(crossed)
            held = [updated, near, far, last]
            others = [(own_other, [0]), (middle_other, [1, 2]), (swap_rep(last), [3])]
            window, settled = [both], [middle_other] if step > 0 else []
        else:
            bits = [1 << i for i in range(n_var.bit_length() - 1)]
            found = {0: updated}
            for bit in reversed(bits):
                for d in list(found):
                    found[d | bit] = shift_var(found[d], bit)
            held = [found[d] for d in range(n_var)]
            sums = dict(enumerate(parts))
            for bit in bits:
                for d in sorted(sums, reverse=True):
                    if d & bit:
                        sums[d ^ bit] = sums[d ^ bit] + wide(
                            shift_var(narrow(sums.pop(d)), bit)
                        )
            summed = sums[0]
            others = [(swap_rep(stack(held)), list(range(n_var)))]
            window, settled = [], []

        if step == 0:
            swapped, entries, _ = swap_all([sent], [sign_labels], [], window)
            jobs = jobs_of(entries)
        else:
            swapped, entries, offset = swap_all(incoming, incoming_labels, [left_own], window)
            tail = [None] * offset + [row_place(1)]
            jobs = jobs_of(entries)
            jobs.append(([(left_own, [row_place(0)]), (swapped, tail)], rows))
        found = list(unpack(meta, jobs))
        unpacked += found
        if step > 0:
            left[0].append(found.pop())
        for index in range(groups):
            right[1 + index].append(found.pop(0))
            left[1 + index].append(right[1 + index][0] if step == 0 else found.pop(0))

        left_own = narrow(wide(tie(left_own, swapped, *settled)) + inverse * summed)
        if step == 2 and n_var == 4:
            incoming = [from_probes(stack(held[:3])), from_probes(stack([last, left_own]))]
            incoming_labels = [[0, 1, 2], [3, "row"]]
        else:
            incoming = [from_probes(stack(held + [left_own]))]
            incoming_labels = [list(range(n_var)) + ["row"]]
        sources = place([(array, [d]) for d, array in enumerate(held)], 0) + place(others, 1)
        if step < 2:
            keep, send = backward(
                meta, cols, other_columns, near_blocks, other_blocks, left_own, blocks, []
            )
            received = swap_rep(send)
            panel, updated = forward(
                meta, cols, other_columns, near_blocks, other_blocks, sources, blocks, inverse,
                [send],
            )
            right[0].append(panel)

    jobs = [(sources, blocks)]
    jobs.append(([(left_own, [row_place(0)]), (swap_rep(left_own), [row_place(1)])], rows))
    ready = list(unpack(meta, jobs))
    right[0].append(ready[0])
    left[0].append(ready[1])
    entries = []
    for array, labels in zip(incoming, incoming_labels):
        tokens = ready + unpacked if array is incoming[-1] else []
        _, entry, _ = swap_all([array], [labels], [], tokens)
        entries += entry
    found = list(unpack(meta, jobs_of(entries)))
    for index in range(groups):
        right[1 + index].append(found.pop(0))
        left[1 + index].append(found.pop(0))

    lefts = [group[t] for t in range(4) for group in left]
    rights = [group[3 - t] for t in range(4) for group in right]
    scale = 1.0 / (count * n_probe)
    return gradient(meta, cols, lefts, rights, rows, slots, scale)


def solution(mesh):
    return jax.shard_map(
        local,
        mesh=mesh,
        in_specs=(
            P(("groups", "var"), "rep", None, None),
            P(("groups", "var"), "rep"),
            P("groups", "probe", None),
        ),
        out_specs=P(("groups", "var"), "rep", None, None),
        check_vma=False,
    )
```

```python
import functools
import math

import jax
import jax.numpy as jnp
from jax import lax
from jax.experimental import pallas as pl
from jax.experimental.pallas import tpu as pltpu
from jax.sharding import PartitionSpec as P

KS = 6
PAD = 16
GRADIENT_ROWS = 8
VMEM_LIMIT = 16 * 1024 * 1024


def whole():
    return pl.BlockSpec(memory_space=pltpu.VMEM)


def params():
    return pltpu.CompilerParams(
        dimension_semantics=("arbitrary",), vmem_limit_bytes=VMEM_LIMIT
    )


def split_pair(pair, count):
    wide = pair.astype(jnp.float32)
    keep = lax.broadcasted_iota(jnp.int32, (PAD, wide.shape[1]), 0) < count
    first = jnp.where(keep, wide[:PAD], 0.0)
    second = jnp.where(keep, pltpu.roll(wide, count, 0)[:PAD], 0.0)
    return first, second


def join_pair(first, second, count):
    tail = jnp.zeros((2 * count - PAD, first.shape[1]), jnp.float32)
    low = jnp.concatenate([first, tail], axis=0)
    high = pltpu.roll(jnp.concatenate([second, tail], axis=0), count, 0)
    return low + high


def anywhere():
    return pl.BlockSpec(memory_space=pl.ANY)


def in_hbm():
    return pl.BlockSpec(memory_space=pltpu.HBM)


def unpack_into(panel, refs, where, count, meta):
    for ref, places in zip(refs, where):
        pairs = ref.shape[1]
        for index, base_of in enumerate(places):
            if base_of is None:
                continue
            base = base_of(meta[0], meta[1])

            def body(i, carry, ref=ref, base=base, index=index):
                first, second = split_pair(ref[index, i], count)
                panel[base + 2 * i] = first.astype(jnp.bfloat16)
                panel[base + 2 * i + 1] = second.astype(jnp.bfloat16)
                return carry

            lax.fori_loop(0, pairs, body, 0, unroll=8 if pairs % 8 == 0 else 4)


def unpack_kernel(count, wheres, skipped, meta, *refs):
    panels = refs[len(refs) - len(wheres) :]
    begin = 0
    for panel, where in zip(panels, wheres):
        unpack_into(panel, refs[begin : begin + len(where)], where, count, meta)
        begin += len(where)


def unpack(meta, jobs, tokens=()):
    arrays = [array for pieces, _ in jobs for array, _ in pieces]
    wheres = [[places for _, places in pieces] for pieces, _ in jobs]
    count = arrays[0].shape[2] // 2
    width = arrays[0].shape[3]
    return pl.pallas_call(
        functools.partial(unpack_kernel, count, wheres, len(tokens)),
        out_shape=[
            jax.ShapeDtypeStruct((blocks, PAD, width), jnp.bfloat16) for _, blocks in jobs
        ],
        grid_spec=pltpu.PrefetchScalarGridSpec(
            num_scalar_prefetch=1,
            grid=(1,),
            in_specs=[whole()] * len(arrays) + [anywhere()] * len(tokens),
            out_specs=[whole()] * len(jobs),
        ),
        compiler_params=params(),
        name="unpack_panels",
    )(meta, *arrays, *tokens)


def row_product(refs_and_rows, panel, contract):
    picked = []
    stored = []
    for ref, row, cols, col_row in refs_and_rows:
        for k in range(ref.shape[1]):
            picked.append(panel[cols[k, col_row]])
            stored.append(ref[row, k])
    return lax.dot_general(
        jnp.concatenate(picked, axis=1),
        jnp.concatenate(stored, axis=1),
        contract,
        preferred_element_type=jnp.float32,
    )


LAST = (((1,), (1,)), ((), ()))
FIRST = (((1,), (0,)), ((), ()))


def first_kernel(
    count, chunk, blocks, meta, cols, signs_hbm, stored,
    panel, sent, mine, keep_row, near, far, keep, send,
    signs, total, sign_sem, sems,
):
    half = near.shape[0]
    rows = 2 * half
    chunks = half // chunk
    rep = lax.axis_index("rep")

    def copy(side, c):
        place = (rep if side == 0 else 1 - rep) * half + c * chunk
        return pltpu.make_async_copy(
            stored.at[pl.ds(place, chunk)],
            (near, far)[side].at[pl.ds(c * chunk, chunk)],
            sems.at[side * chunks + c],
        )

    sign_copy = pltpu.make_async_copy(signs_hbm, signs, sign_sem)
    sign_copy.start()
    for side in (0, 1):
        for c in range(chunks):
            copy(side, c).start()
    total[...] = jnp.zeros_like(total)
    sign_copy.wait()
    pad = jnp.zeros((PAD - count, signs.shape[1]), jnp.float32)

    def convert(b, carry):
        value = signs[pl.ds(b, count, stride=blocks), :].astype(jnp.float32)
        panel[b] = jnp.concatenate([value, pad], axis=0).astype(jnp.bfloat16)
        return carry

    lax.fori_loop(0, blocks, convert, 0, unroll=8)
    first_block = meta[0] * rows
    for side, ref in ((0, near), (1, far)):
        offset = meta[1] * half if side == 0 else (1 - meta[1]) * half

        def body(c, carry, side=side, ref=ref, offset=offset):
            copy(side, c).wait()
            row = c * chunk
            for i in range(0, chunk, 2):
                results = [
                    row_product([(ref, row + r, cols, offset + row + r)], panel, LAST)
                    for r in (i, i + 1)
                ]
                pair = join_pair(results[0], results[1], count)
                if side == 0:
                    keep_row[(row + i) // 2] = pair
                else:
                    send[send.shape[0] - 1, (row + i) // 2] = pair.astype(jnp.bfloat16)
                for r in (i, i + 1):
                    scatter_row(
                        panel[first_block + offset + row + r],
                        [(ref, row + r, cols, offset + row + r)],
                        total,
                    )
            return carry

        lax.fori_loop(0, chunks, body, 0)
    parts, pair_rows = sent.shape[0], sent.shape[1]
    for start, out, index in [
        (meta[1] * (blocks // 2) + p * 2 * pair_rows, sent, p) for p in range(parts)
    ] + [(first_block + meta[1] * half, mine, 0)]:

        def pack(i, carry, start=start, out=out, index=index):
            b = start + 2 * i
            out[index, i] = join_pair(
                panel[b].astype(jnp.float32), panel[b + 1].astype(jnp.float32), count
            ).astype(jnp.bfloat16)
            return carry

        lax.fori_loop(0, pair_rows, pack, 0, unroll=8 if pair_rows % 8 == 0 else 4)
    give_totals(count, rows, meta, keep, send, total)


def first_step(meta, cols, signs, stored, blocks):
    rows, slots, width = stored.shape[0], stored.shape[1], stored.shape[3]
    count = signs.shape[0] // blocks
    half = rows // 2
    chunk = min(32, half)
    parts = blocks // rows
    shape = jax.ShapeDtypeStruct
    piece = (half // 2, 2 * count, width)
    return pl.pallas_call(
        functools.partial(first_kernel, count, chunk, blocks),
        out_shape=(
            shape((blocks, PAD, width), jnp.bfloat16),
            shape((parts,) + piece, jnp.bfloat16),
            shape((1,) + piece, jnp.bfloat16),
            shape(piece, jnp.float32),
            shape((half, slots, width, width), jnp.bfloat16),
            shape((half, slots, width, width), jnp.bfloat16),
            shape((parts,) + piece, jnp.bfloat16),
            shape((parts + 1,) + piece, jnp.bfloat16),
        ),
        grid_spec=pltpu.PrefetchScalarGridSpec(
            num_scalar_prefetch=2,
            grid=(1,),
            in_specs=[in_hbm(), in_hbm()],
            out_specs=(whole(),) * 8,
            scratch_shapes=[
                pltpu.VMEM(signs.shape, jnp.int32),
                pltpu.VMEM((blocks, PAD, width), jnp.float32),
                pltpu.SemaphoreType.DMA(()),
                pltpu.SemaphoreType.DMA((2 * half // chunk,)),
            ],
        ),
        compiler_params=params(),
        cost_estimate=cost(2 * rows * slots, width),
        name="first_step",
    )(meta, cols, signs, stored)


def cost(stored, width):
    return pl.CostEstimate(
        flops=2 * stored * 128 * width * width,
        transcendentals=0,
        bytes_accessed=8 * stored * width * width,
    )


def forward_kernel(
    count, chunk, rows, inverse, where, meta, cols_own, cols_other, own, other, *rest
):
    panel, out = rest[-2:]
    unpack_into(panel, rest[: len(where)], where, count, meta)
    half = rows // 2
    block = meta[0] * rows + meta[1] * half

    def body(step, carry):
        row = step * chunk
        for i in range(0, chunk, 2):
            results = []
            for r in (i, i + 1):
                product = row_product(
                    [
                        (own, row + r, cols_own, meta[1] * half + row + r),
                        (other, row + r, cols_other, meta[1] * half + row + r),
                    ],
                    panel,
                    LAST,
                )
                results.append(panel[block + row + r].astype(jnp.float32) + inverse * product)
            out[0, (row + i) // 2] = join_pair(results[0], results[1], count).astype(
                jnp.bfloat16
            )
        return carry

    lax.fori_loop(0, half // chunk, body, 0)


def forward(meta, cols_own, cols_other, own, other, pieces, blocks, inverse, tokens):
    half, slots, width = own.shape[0], own.shape[1], own.shape[3]
    arrays = [array for array, _ in pieces]
    count = arrays[0].shape[2] // 2
    chunk = min(32, half)
    return pl.pallas_call(
        functools.partial(
            forward_kernel, count, chunk, 2 * half, inverse, [places for _, places in pieces]
        ),
        out_shape=(
            jax.ShapeDtypeStruct((blocks, PAD, width), jnp.bfloat16),
            jax.ShapeDtypeStruct((1, half // 2, 2 * count, width), jnp.bfloat16),
        ),
        grid_spec=pltpu.PrefetchScalarGridSpec(
            num_scalar_prefetch=3,
            grid=(1,),
            in_specs=[whole()] * (2 + len(arrays)) + [anywhere()] * len(tokens),
            out_specs=(whole(), whole()),
        ),
        compiler_params=params(),
        cost_estimate=cost(2 * half * slots, width),
        name="forward_step",
    )(meta, cols_own, cols_other, own, other, *arrays, *tokens)


def scatter_row(value, refs_and_rows, total):
    targets = []
    stored = []
    for ref, row, cols, col_row in refs_and_rows:
        for k in range(ref.shape[1]):
            targets.append(cols[k, col_row])
            stored.append(ref[row, k])
    terms = lax.dot_general(
        value, jnp.concatenate(stored, axis=1), FIRST, preferred_element_type=jnp.float32
    )
    width = stored[0].shape[1]
    for i, target in enumerate(targets):
        total[target] = total[target] + terms[:, i * width : (i + 1) * width]


def give_totals(count, rows, meta, keep, send, total):
    half = rows // 2
    pairs = half // 2
    for out, h in ((send, 1), (keep, 0)):
        for d in range(keep.shape[0]):
            base = (meta[0] ^ d) * rows + (meta[1] ^ h) * half

            def body(i, carry, out=out, base=base, d=d):
                out[d, i] = join_pair(
                    total[base + 2 * i], total[base + 2 * i + 1], count
                ).astype(jnp.bfloat16)
                return carry

            lax.fori_loop(0, pairs, body, 0, unroll=8 if pairs % 8 == 0 else 4)


def backward_kernel(
    count, chunk, meta, cols_own, cols_other, own, other, left, *rest
):
    keep, send, total = rest[-3:]
    half = own.shape[0]
    stored = ((own, cols_own), (other, cols_other))
    total[...] = jnp.zeros_like(total)

    def body(step, carry):
        for i in range(0, chunk, 2):
            pair = split_pair(left[0, (step * chunk + i) // 2], count)
            for r, value in zip((i, i + 1), pair):
                row = step * chunk + r
                scatter_row(
                    value.astype(jnp.bfloat16),
                    [(ref, row, cols, meta[1] * half + row) for ref, cols in stored],
                    total,
                )
        return carry

    lax.fori_loop(0, half // chunk, body, 0)
    give_totals(count, 2 * half, meta, keep, send, total)


def backward(meta, cols_own, cols_other, own, other, left, blocks, tokens):
    half, slots, width = own.shape[0], own.shape[1], own.shape[3]
    count = left.shape[2] // 2
    chunk = min(32, half)
    result = jax.ShapeDtypeStruct(
        (blocks // (2 * half), half // 2, 2 * count, width), jnp.bfloat16
    )
    return pl.pallas_call(
        functools.partial(backward_kernel, count, chunk),
        out_shape=(result, result),
        grid_spec=pltpu.PrefetchScalarGridSpec(
            num_scalar_prefetch=3,
            grid=(1,),
            in_specs=[whole()] * 3 + [anywhere()] * len(tokens),
            out_specs=(whole(), whole()),
            scratch_shapes=[pltpu.VMEM((blocks, PAD, width), jnp.float32)],
        ),
        compiler_params=params(),
        cost_estimate=cost(2 * half * slots, width),
        name="backward_step",
    )(meta, cols_own, cols_other, own, other, left, *tokens)


def gradient_kernel(scale, chunk, rows, terms, meta, cols, *refs):
    out, made, sems = refs[-3:]
    lefts = refs[: 4 * terms]
    rights = refs[4 * terms : 8 * terms]
    slots, width = out.shape[1], out.shape[3]
    contract = (((0,), (0,)), ((), ()))

    def copy(step):
        part = pl.ds(step * chunk, chunk)
        return pltpu.make_async_copy(made.at[part], out.at[part], sems.at[step])

    def body(step, carry):
        for r in range(chunk):
            row = step * chunk + r
            left = []
            for position, ref in enumerate(lefts):
                start = meta[0] * rows if position < terms else 0
                left.append(ref[start + row])
            left = jnp.concatenate(left, axis=0)
            right = []
            for k in range(slots):
                target = cols[k, row]
                right.append(jnp.concatenate([ref[target] for ref in rights], axis=0))
            product = lax.dot_general(
                left, jnp.concatenate(right, axis=1), contract, preferred_element_type=jnp.float32
            )
            for k in range(slots):
                made[row, k] = (product[:, k * width : (k + 1) * width] * scale).astype(
                    jnp.bfloat16
                )
        copy(step).start()
        return carry

    for step in range(rows // chunk):
        body(step, 0)
    for step in range(rows // chunk):
        copy(step).wait()


def gradient(meta, cols, lefts, rights, rows, slots, scale):
    width = lefts[0].shape[2]
    chunk = min(GRADIENT_ROWS, rows)
    operands = list(lefts) + list(rights)
    shape = (rows, slots, width, width)
    return pl.pallas_call(
        functools.partial(gradient_kernel, scale, chunk, rows, len(lefts) // 4),
        out_shape=jax.ShapeDtypeStruct(shape, jnp.bfloat16),
        grid_spec=pltpu.PrefetchScalarGridSpec(
            num_scalar_prefetch=2,
            grid=(1,),
            in_specs=[whole()] * len(operands),
            out_specs=anywhere(),
            scratch_shapes=[
                pltpu.VMEM(shape, jnp.bfloat16),
                pltpu.SemaphoreType.DMA((rows // chunk,)),
            ],
        ),
        compiler_params=params(),
        name="gradient",
    )(meta, cols, *operands)


def tie(x, *tokens):
    return lax.optimization_barrier((x,) + tokens)[0]


def local(block_values, columns, probe_signs):
    rows, slots, width = block_values.shape[0], block_values.shape[1], block_values.shape[3]
    blocks, count = probe_signs.shape[0], probe_signs.shape[1]
    half = rows // 2
    n_var = lax.axis_size("var")
    n_probe = lax.axis_size("probe")
    groups = n_probe - 1
    inverse = 1.0 / math.sqrt(KS * width)
    meta = jnp.stack([lax.axis_index("var"), lax.axis_index("rep")]).astype(jnp.int32)
    signs = jnp.transpose(probe_signs, (1, 0, 2)).reshape(count * blocks, width)
    signs = pltpu.with_memory_space_constraint(signs, pltpu.HBM)
    block_values = pltpu.with_memory_space_constraint(block_values, pltpu.HBM)
    cols = columns.T
    cols_hbm = pltpu.with_memory_space_constraint(cols, pltpu.HBM)

    def swap_rep(x):
        return lax.ppermute(x, "rep", [(0, 1), (1, 0)])

    def shift_var(x, bit):
        return lax.ppermute(x, "var", [(i, i ^ bit) for i in range(n_var)])

    def from_probes(x):
        return stack(
            [
                lax.ppermute(x, "probe", [(i, (i + d) % n_probe) for i in range(n_probe)])
                for d in range(1, n_probe)
            ]
        )

    def stack(arrays):
        return arrays[0] if len(arrays) == 1 else jnp.concatenate(arrays, axis=0)

    def wide(x):
        return x.astype(jnp.float32)

    def narrow(x):
        return x.astype(jnp.bfloat16)

    def home(d, h):
        return lambda v, r: (v ^ d) * rows + (r ^ h) * half

    def row_place(h):
        return lambda v, r: (r ^ h) * half

    def sign_place(p, h):
        return lambda v, r: (r ^ h) * (blocks // 2) + p * half

    def spot(label, h):
        if label == "row":
            return row_place(h)
        return home(label, h) if label < n_var else sign_place(label - n_var, h)

    def place(pieces, h):
        return [
            (array, [None if d is None else home(d, h) for d in ds]) for array, ds in pieces
        ]

    def jobs_of(entries):
        jobs = []
        for index in range(groups):
            for kind in ("blocks", "rows"):
                pieces = []
                for h in (0, 1):
                    for here, swapped, offset, labels in entries:
                        array, skip = (here, 0) if h == 0 else (swapped, offset)
                        where = [None] * array.shape[0]
                        for i, label in enumerate(labels):
                            if (label == "row") == (kind == "rows"):
                                where[skip + index * len(labels) + i] = spot(label, h)
                        if any(base is not None for base in where):
                            pieces.append((array, where))
                if pieces:
                    jobs.append((pieces, blocks if kind == "blocks" else rows))
        return jobs

    def swap_all(arrays, labels, extra, tokens):
        joined = list(arrays) + list(extra)
        if tokens:
            joined = [tie(array, *tokens) for array in joined]
        swapped = swap_rep(stack(joined))
        entries = []
        offset = 0
        for array, names in zip(arrays, labels):
            entries.append((array, swapped, offset, names))
            offset += array.shape[0]
        return swapped, entries, offset

    panel, sent, left_own, kept, near_blocks, far_blocks, keep, send = first_step(
        meta, cols_hbm, signs, block_values, blocks
    )
    received = swap_rep(send)
    updated = narrow(wide(left_own) + inverse * (kept + wide(received[n_var]))[None])
    other_blocks = swap_rep(tie(far_blocks, updated))
    other_columns = swap_rep(cols)
    right = [[panel]] + [[] for _ in range(groups)]
    left = [[panel]] + [[] for _ in range(groups)]
    sent = from_probes(tie(sent, updated))
    sign_labels = [n_var + p for p in range(n_var)]
    incoming, incoming_labels = [], []
    unpacked = []

    for step in range(3):
        parts = [wide(keep[d : d + 1]) + wide(received[d : d + 1]) for d in range(n_var)]
        if n_var == 4:
            far = shift_var(updated, 2)
            both = shift_var(stack([updated, narrow(parts[3])]), 1)
            near = both[:1]
            crossed = shift_var(narrow(parts[2] + wide(both[1:])), 2)
            final = shift_var(stack([far, narrow(parts[1])]), 1)
            last = final[:1]
            middle_other = swap_rep(stack([updated, near, far]))
            summed = parts[0] + wide(final[1:]) + wide(crossed)
            held = [updated, near, far, last]
            others = [(middle_other, [0, 1, 2]), (swap_rep(last), [3])]
            window, settled = [both], [middle_other] if step > 0 else []
        else:
            bits = [1 << i for i in range(n_var.bit_length() - 1)]
            found = {0: updated}
            for bit in reversed(bits):
                for d in list(found):
                    found[d | bit] = shift_var(found[d], bit)
            held = [found[d] for d in range(n_var)]
            sums = dict(enumerate(parts))
            for bit in bits:
                for d in sorted(sums, reverse=True):
                    if d & bit:
                        sums[d ^ bit] = sums[d ^ bit] + wide(
                            shift_var(narrow(sums.pop(d)), bit)
                        )
            summed = sums[0]
            others = [(swap_rep(stack(held)), list(range(n_var)))]
            window, settled = [], []

        if step == 0:
            swapped, entries, _ = swap_all([sent], [sign_labels], [], window)
            jobs = jobs_of(entries)
        else:
            swapped, entries, offset = swap_all(incoming, incoming_labels, [left_own], window)
            tail = [None] * offset + [row_place(1)]
            jobs = jobs_of(entries)
            jobs.append(([(left_own, [row_place(0)]), (swapped, tail)], rows))
        found = list(unpack(meta, jobs))
        unpacked += found
        if step > 0:
            left[0].append(found.pop())
        for index in range(groups):
            right[1 + index].append(found.pop(0))
            left[1 + index].append(right[1 + index][0] if step == 0 else found.pop(0))

        left_own = narrow(wide(tie(left_own, swapped, *settled)) + inverse * summed)
        if step == 2 and n_var == 4:
            incoming = [from_probes(stack(held[:3])), from_probes(stack([last, left_own]))]
            incoming_labels = [[0, 1, 2], [3, "row"]]
        else:
            incoming = [from_probes(stack(held + [left_own]))]
            incoming_labels = [list(range(n_var)) + ["row"]]
        sources = place([(array, [d]) for d, array in enumerate(held)], 0) + place(others, 1)
        if step < 2:
            keep, send = backward(
                meta, cols, other_columns, near_blocks, other_blocks, left_own, blocks, []
            )
            received = swap_rep(send)
            panel, updated = forward(
                meta, cols, other_columns, near_blocks, other_blocks, sources, blocks, inverse,
                [send],
            )
            right[0].append(panel)

    jobs = [(sources, blocks)]
    jobs.append(([(left_own, [row_place(0)]), (swap_rep(left_own), [row_place(1)])], rows))
    ready = list(unpack(meta, jobs))
    right[0].append(ready[0])
    left[0].append(ready[1])
    entries = []
    for array, labels in zip(incoming, incoming_labels):
        tokens = ready + unpacked if array is incoming[-1] else []
        _, entry, _ = swap_all([array], [labels], [], tokens)
        entries += entry
    found = list(unpack(meta, jobs_of(entries)))
    for index in range(groups):
        right[1 + index].append(found.pop(0))
        left[1 + index].append(found.pop(0))

    lefts = [group[t] for t in range(4) for group in left]
    rights = [group[3 - t] for t in range(4) for group in right]
    scale = 1.0 / (count * n_probe)
    return gradient(meta, cols, lefts, rights, rows, slots, scale)


def solution(mesh):
    return jax.shard_map(
        local,
        mesh=mesh,
        in_specs=(
            P(("groups", "var"), "rep", None, None),
            P(("groups", "var"), "rep"),
            P("groups", "probe", None),
        ),
        out_specs=P(("groups", "var"), "rep", None, None),
        check_vma=False,
    )
```

```python
import functools
import math

import jax
import jax.numpy as jnp
from jax import lax
from jax.experimental import pallas as pl
from jax.experimental.pallas import tpu as pltpu
from jax.sharding import PartitionSpec as P

KS = 6
PAD = 16
GRADIENT_ROWS = 8
VMEM_LIMIT = 16 * 1024 * 1024


def whole():
    return pl.BlockSpec(memory_space=pltpu.VMEM)


def params():
    return pltpu.CompilerParams(
        dimension_semantics=("arbitrary",), vmem_limit_bytes=VMEM_LIMIT
    )


def split_pair(pair, count):
    wide = pair.astype(jnp.float32)
    keep = lax.broadcasted_iota(jnp.int32, (PAD, wide.shape[1]), 0) < count
    first = jnp.where(keep, wide[:PAD], 0.0)
    second = jnp.where(keep, pltpu.roll(wide, count, 0)[:PAD], 0.0)
    return first, second


def join_pair(first, second, count):
    tail = jnp.zeros((2 * count - PAD, first.shape[1]), jnp.float32)
    low = jnp.concatenate([first, tail], axis=0)
    high = pltpu.roll(jnp.concatenate([second, tail], axis=0), count, 0)
    return low + high


def anywhere():
    return pl.BlockSpec(memory_space=pl.ANY)


def in_hbm():
    return pl.BlockSpec(memory_space=pltpu.HBM)


def unpack_into(panel, refs, where, count, meta):
    for ref, places in zip(refs, where):
        pairs = ref.shape[1]
        for index, base_of in enumerate(places):
            if base_of is None:
                continue
            base = base_of(meta[0], meta[1])

            def body(i, carry, ref=ref, base=base, index=index):
                first, second = split_pair(ref[index, i], count)
                panel[base + 2 * i] = first.astype(jnp.bfloat16)
                panel[base + 2 * i + 1] = second.astype(jnp.bfloat16)
                return carry

            lax.fori_loop(0, pairs, body, 0, unroll=8 if pairs % 8 == 0 else 4)


def unpack_kernel(count, wheres, skipped, meta, *refs):
    panels = refs[len(refs) - len(wheres) :]
    begin = 0
    for panel, where in zip(panels, wheres):
        unpack_into(panel, refs[begin : begin + len(where)], where, count, meta)
        begin += len(where)


def unpack(meta, jobs, tokens=()):
    arrays = [array for pieces, _ in jobs for array, _ in pieces]
    wheres = [[places for _, places in pieces] for pieces, _ in jobs]
    count = arrays[0].shape[2] // 2
    width = arrays[0].shape[3]
    return pl.pallas_call(
        functools.partial(unpack_kernel, count, wheres, len(tokens)),
        out_shape=[
            jax.ShapeDtypeStruct((blocks, PAD, width), jnp.bfloat16) for _, blocks in jobs
        ],
        grid_spec=pltpu.PrefetchScalarGridSpec(
            num_scalar_prefetch=1,
            grid=(1,),
            in_specs=[whole()] * len(arrays) + [anywhere()] * len(tokens),
            out_specs=[whole()] * len(jobs),
        ),
        compiler_params=params(),
        name="unpack_panels",
    )(meta, *arrays, *tokens)


def row_product(refs_and_rows, panel, contract):
    picked = []
    stored = []
    for ref, row, cols, col_row in refs_and_rows:
        for k in range(ref.shape[1]):
            picked.append(panel[cols[k, col_row]])
            stored.append(ref[row, k])
    return lax.dot_general(
        jnp.concatenate(picked, axis=1),
        jnp.concatenate(stored, axis=1),
        contract,
        preferred_element_type=jnp.float32,
    )


LAST = (((1,), (1,)), ((), ()))
FIRST = (((1,), (0,)), ((), ()))


def first_kernel(
    count, chunk, blocks, meta, cols, signs_hbm, stored,
    panel, sent, mine, keep_row, near, far, keep, send,
    signs, total, sign_sem, sems,
):
    half = near.shape[0]
    rows = 2 * half
    chunks = half // chunk
    rep = lax.axis_index("rep")

    def copy(side, c):
        place = (rep if side == 0 else 1 - rep) * half + c * chunk
        return pltpu.make_async_copy(
            stored.at[pl.ds(place, chunk)],
            (near, far)[side].at[pl.ds(c * chunk, chunk)],
            sems.at[side * chunks + c],
        )

    sign_copy = pltpu.make_async_copy(signs_hbm, signs, sign_sem)
    sign_copy.start()
    for side in (0, 1):
        for c in range(chunks):
            copy(side, c).start()
    total[...] = jnp.zeros_like(total)
    sign_copy.wait()
    pad = jnp.zeros((PAD - count, signs.shape[1]), jnp.float32)

    def convert(b, carry):
        value = signs[pl.ds(b, count, stride=blocks), :].astype(jnp.float32)
        panel[b] = jnp.concatenate([value, pad], axis=0).astype(jnp.bfloat16)
        return carry

    lax.fori_loop(0, blocks, convert, 0, unroll=8)
    first_block = meta[0] * rows
    for side, ref in ((0, near), (1, far)):
        offset = meta[1] * half if side == 0 else (1 - meta[1]) * half

        def body(c, carry, side=side, ref=ref, offset=offset):
            copy(side, c).wait()
            row = c * chunk
            for i in range(0, chunk, 2):
                results = [
                    row_product([(ref, row + r, cols, offset + row + r)], panel, LAST)
                    for r in (i, i + 1)
                ]
                pair = join_pair(results[0], results[1], count)
                if side == 0:
                    keep_row[(row + i) // 2] = pair
                else:
                    send[send.shape[0] - 1, (row + i) // 2] = pair.astype(jnp.bfloat16)
                for r in (i, i + 1):
                    scatter_row(
                        panel[first_block + offset + row + r],
                        [(ref, row + r, cols, offset + row + r)],
                        total,
                    )
            return carry

        lax.fori_loop(0, chunks, body, 0)
    parts, pair_rows = sent.shape[0], sent.shape[1]
    for start, out, index in [
        (meta[1] * (blocks // 2) + p * 2 * pair_rows, sent, p) for p in range(parts)
    ] + [(first_block + meta[1] * half, mine, 0)]:

        def pack(i, carry, start=start, out=out, index=index):
            b = start + 2 * i
            out[index, i] = join_pair(
                panel[b].astype(jnp.float32), panel[b + 1].astype(jnp.float32), count
            ).astype(jnp.bfloat16)
            return carry

        lax.fori_loop(0, pair_rows, pack, 0, unroll=8 if pair_rows % 8 == 0 else 4)
    give_totals(count, rows, meta, keep, send, total)


def first_step(meta, cols, signs, stored, blocks):
    rows, slots, width = stored.shape[0], stored.shape[1], stored.shape[3]
    count = signs.shape[0] // blocks
    half = rows // 2
    chunk = min(32, half)
    parts = blocks // rows
    shape = jax.ShapeDtypeStruct
    piece = (half // 2, 2 * count, width)
    return pl.pallas_call(
        functools.partial(first_kernel, count, chunk, blocks),
        out_shape=(
            shape((blocks, PAD, width), jnp.bfloat16),
            shape((parts,) + piece, jnp.bfloat16),
            shape((1,) + piece, jnp.bfloat16),
            shape(piece, jnp.float32),
            shape((half, slots, width, width), jnp.bfloat16),
            shape((half, slots, width, width), jnp.bfloat16),
            shape((parts,) + piece, jnp.bfloat16),
            shape((parts + 1,) + piece, jnp.bfloat16),
        ),
        grid_spec=pltpu.PrefetchScalarGridSpec(
            num_scalar_prefetch=2,
            grid=(1,),
            in_specs=[in_hbm(), in_hbm()],
            out_specs=(whole(),) * 8,
            scratch_shapes=[
                pltpu.VMEM(signs.shape, jnp.int32),
                pltpu.VMEM((blocks, PAD, width), jnp.float32),
                pltpu.SemaphoreType.DMA(()),
                pltpu.SemaphoreType.DMA((2 * half // chunk,)),
            ],
        ),
        compiler_params=params(),
        cost_estimate=cost(2 * rows * slots, width),
        name="first_step",
    )(meta, cols, signs, stored)


def cost(stored, width):
    return pl.CostEstimate(
        flops=2 * stored * 128 * width * width,
        transcendentals=0,
        bytes_accessed=8 * stored * width * width,
    )


def forward_kernel(
    count, chunk, rows, inverse, where, meta, cols_own, cols_other, own, other, *rest
):
    panel, out = rest[-2:]
    unpack_into(panel, rest[: len(where)], where, count, meta)
    half = rows // 2
    block = meta[0] * rows + meta[1] * half

    def body(step, carry):
        row = step * chunk
        for i in range(0, chunk, 2):
            results = []
            for r in (i, i + 1):
                product = row_product(
                    [
                        (own, row + r, cols_own, meta[1] * half + row + r),
                        (other, row + r, cols_other, meta[1] * half + row + r),
                    ],
                    panel,
                    LAST,
                )
                results.append(panel[block + row + r].astype(jnp.float32) + inverse * product)
            out[0, (row + i) // 2] = join_pair(results[0], results[1], count).astype(
                jnp.bfloat16
            )
        return carry

    lax.fori_loop(0, half // chunk, body, 0)


def forward(meta, cols_own, cols_other, own, other, pieces, blocks, inverse, tokens):
    half, slots, width = own.shape[0], own.shape[1], own.shape[3]
    arrays = [array for array, _ in pieces]
    count = arrays[0].shape[2] // 2
    chunk = min(32, half)
    return pl.pallas_call(
        functools.partial(
            forward_kernel, count, chunk, 2 * half, inverse, [places for _, places in pieces]
        ),
        out_shape=(
            jax.ShapeDtypeStruct((blocks, PAD, width), jnp.bfloat16),
            jax.ShapeDtypeStruct((1, half // 2, 2 * count, width), jnp.bfloat16),
        ),
        grid_spec=pltpu.PrefetchScalarGridSpec(
            num_scalar_prefetch=3,
            grid=(1,),
            in_specs=[whole()] * (2 + len(arrays)) + [anywhere()] * len(tokens),
            out_specs=(whole(), whole()),
        ),
        compiler_params=params(),
        cost_estimate=cost(2 * half * slots, width),
        name="forward_step",
    )(meta, cols_own, cols_other, own, other, *arrays, *tokens)


def scatter_row(value, refs_and_rows, total):
    targets = []
    stored = []
    for ref, row, cols, col_row in refs_and_rows:
        for k in range(ref.shape[1]):
            targets.append(cols[k, col_row])
            stored.append(ref[row, k])
    terms = lax.dot_general(
        value, jnp.concatenate(stored, axis=1), FIRST, preferred_element_type=jnp.float32
    )
    width = stored[0].shape[1]
    for i, target in enumerate(targets):
        total[target] = total[target] + terms[:, i * width : (i + 1) * width]


def give_totals(count, rows, meta, keep, send, total):
    half = rows // 2
    pairs = half // 2
    for out, h in ((send, 1), (keep, 0)):
        for d in range(keep.shape[0]):
            base = (meta[0] ^ d) * rows + (meta[1] ^ h) * half

            def body(i, carry, out=out, base=base, d=d):
                out[d, i] = join_pair(
                    total[base + 2 * i], total[base + 2 * i + 1], count
                ).astype(jnp.bfloat16)
                return carry

            lax.fori_loop(0, pairs, body, 0, unroll=8 if pairs % 8 == 0 else 4)


def backward_kernel(
    count, chunk, meta, cols_own, cols_other, own, other, left, *rest
):
    keep, send, total = rest[-3:]
    half = own.shape[0]
    stored = ((own, cols_own), (other, cols_other))
    total[...] = jnp.zeros_like(total)

    def body(step, carry):
        for i in range(0, chunk, 2):
            pair = split_pair(left[0, (step * chunk + i) // 2], count)
            for r, value in zip((i, i + 1), pair):
                row = step * chunk + r
                scatter_row(
                    value.astype(jnp.bfloat16),
                    [(ref, row, cols, meta[1] * half + row) for ref, cols in stored],
                    total,
                )
        return carry

    lax.fori_loop(0, half // chunk, body, 0)
    give_totals(count, 2 * half, meta, keep, send, total)


def backward(meta, cols_own, cols_other, own, other, left, blocks, tokens):
    half, slots, width = own.shape[0], own.shape[1], own.shape[3]
    count = left.shape[2] // 2
    chunk = min(32, half)
    result = jax.ShapeDtypeStruct(
        (blocks // (2 * half), half // 2, 2 * count, width), jnp.bfloat16
    )
    return pl.pallas_call(
        functools.partial(backward_kernel, count, chunk),
        out_shape=(result, result),
        grid_spec=pltpu.PrefetchScalarGridSpec(
            num_scalar_prefetch=3,
            grid=(1,),
            in_specs=[whole()] * 3 + [anywhere()] * len(tokens),
            out_specs=(whole(), whole()),
            scratch_shapes=[pltpu.VMEM((blocks, PAD, width), jnp.float32)],
        ),
        compiler_params=params(),
        cost_estimate=cost(2 * half * slots, width),
        name="backward_step",
    )(meta, cols_own, cols_other, own, other, left, *tokens)


def gradient_kernel(scale, chunk, rows, terms, meta, cols, *refs):
    out, made, sems = refs[-3:]
    lefts = refs[: 4 * terms]
    rights = refs[4 * terms : 8 * terms]
    slots, width = out.shape[1], out.shape[3]
    contract = (((0,), (0,)), ((), ()))

    def copy(step):
        part = pl.ds(step * chunk, chunk)
        return pltpu.make_async_copy(made.at[part], out.at[part], sems.at[step])

    def body(step, carry):
        for r in range(chunk):
            row = step * chunk + r
            left = []
            for position, ref in enumerate(lefts):
                start = meta[0] * rows if position < terms else 0
                left.append(ref[start + row])
            left = jnp.concatenate(left, axis=0)
            right = []
            for k in range(slots):
                target = cols[k, row]
                right.append(jnp.concatenate([ref[target] for ref in rights], axis=0))
            product = lax.dot_general(
                left, jnp.concatenate(right, axis=1), contract, preferred_element_type=jnp.float32
            )
            for k in range(slots):
                made[row, k] = (product[:, k * width : (k + 1) * width] * scale).astype(
                    jnp.bfloat16
                )
        copy(step).start()
        return carry

    for step in range(rows // chunk):
        body(step, 0)
    for step in range(rows // chunk):
        copy(step).wait()


def gradient(meta, cols, lefts, rights, rows, slots, scale):
    width = lefts[0].shape[2]
    chunk = min(GRADIENT_ROWS, rows)
    operands = list(lefts) + list(rights)
    shape = (rows, slots, width, width)
    return pl.pallas_call(
        functools.partial(gradient_kernel, scale, chunk, rows, len(lefts) // 4),
        out_shape=jax.ShapeDtypeStruct(shape, jnp.bfloat16),
        grid_spec=pltpu.PrefetchScalarGridSpec(
            num_scalar_prefetch=2,
            grid=(1,),
            in_specs=[whole()] * len(operands),
            out_specs=anywhere(),
            scratch_shapes=[
                pltpu.VMEM(shape, jnp.bfloat16),
                pltpu.SemaphoreType.DMA((rows // chunk,)),
            ],
        ),
        compiler_params=params(),
        name="gradient",
    )(meta, cols, *operands)


def tie(x, *tokens):
    return lax.optimization_barrier((x,) + tokens)[0]


def local(block_values, columns, probe_signs):
    rows, slots, width = block_values.shape[0], block_values.shape[1], block_values.shape[3]
    blocks, count = probe_signs.shape[0], probe_signs.shape[1]
    half = rows // 2
    n_var = lax.axis_size("var")
    n_probe = lax.axis_size("probe")
    groups = n_probe - 1
    inverse = 1.0 / math.sqrt(KS * width)
    meta = jnp.stack([lax.axis_index("var"), lax.axis_index("rep")]).astype(jnp.int32)
    signs = jnp.transpose(probe_signs, (1, 0, 2)).reshape(count * blocks, width)
    signs = pltpu.with_memory_space_constraint(signs, pltpu.HBM)
    block_values = pltpu.with_memory_space_constraint(block_values, pltpu.HBM)
    cols = columns.T
    cols_hbm = pltpu.with_memory_space_constraint(cols, pltpu.HBM)

    def swap_rep(x):
        return lax.ppermute(x, "rep", [(0, 1), (1, 0)])

    def shift_var(x, bit):
        return lax.ppermute(x, "var", [(i, i ^ bit) for i in range(n_var)])

    def from_probes(x):
        return stack(
            [
                lax.ppermute(x, "probe", [(i, (i + d) % n_probe) for i in range(n_probe)])
                for d in range(1, n_probe)
            ]
        )

    def stack(arrays):
        return arrays[0] if len(arrays) == 1 else jnp.concatenate(arrays, axis=0)

    def wide(x):
        return x.astype(jnp.float32)

    def narrow(x):
        return x.astype(jnp.bfloat16)

    def home(d, h):
        return lambda v, r: (v ^ d) * rows + (r ^ h) * half

    def row_place(h):
        return lambda v, r: (r ^ h) * half

    def sign_place(p, h):
        return lambda v, r: (r ^ h) * (blocks // 2) + p * half

    def spot(label, h):
        if label == "row":
            return row_place(h)
        return home(label, h) if label < n_var else sign_place(label - n_var, h)

    def place(pieces, h):
        return [
            (array, [None if d is None else home(d, h) for d in ds]) for array, ds in pieces
        ]

    def jobs_of(entries):
        jobs = []
        for index in range(groups):
            for kind in ("blocks", "rows"):
                pieces = []
                for h in (0, 1):
                    for here, swapped, offset, labels in entries:
                        array, skip = (here, 0) if h == 0 else (swapped, offset)
                        where = [None] * array.shape[0]
                        for i, label in enumerate(labels):
                            if (label == "row") == (kind == "rows"):
                                where[skip + index * len(labels) + i] = spot(label, h)
                        if any(base is not None for base in where):
                            pieces.append((array, where))
                if pieces:
                    jobs.append((pieces, blocks if kind == "blocks" else rows))
        return jobs

    def swap_all(arrays, labels, extra, tokens):
        joined = list(arrays) + list(extra)
        if tokens:
            joined = [tie(array, *tokens) for array in joined]
        swapped = swap_rep(stack(joined))
        entries = []
        offset = 0
        for array, names in zip(arrays, labels):
            entries.append((array, swapped, offset, names))
            offset += array.shape[0]
        return swapped, entries, offset

    panel, sent, left_own, kept, near_blocks, far_blocks, keep, send = first_step(
        meta, cols_hbm, signs, block_values, blocks
    )
    received = swap_rep(send)
    updated = narrow(wide(left_own) + inverse * (kept + wide(received[n_var]))[None])
    other_blocks = swap_rep(tie(far_blocks, updated))
    other_columns = swap_rep(cols)
    right = [[panel]] + [[] for _ in range(groups)]
    left = [[panel]] + [[] for _ in range(groups)]
    sent = from_probes(tie(sent, updated))
    sign_labels = [n_var + p for p in range(n_var)]
    incoming, incoming_labels = [], []
    unpacked = []

    for step in range(3):
        parts = [wide(keep[d : d + 1]) + wide(received[d : d + 1]) for d in range(n_var)]
        if n_var == 4:
            far = shift_var(updated, 2)
            both = shift_var(stack([updated, narrow(parts[3])]), 1)
            near = both[:1]
            third = narrow(parts[2] + wide(both[1:]))
            crossed = shift_var(third, 2)
            pair = stack([far, narrow(parts[1])])
            final = shift_var(pair, 1)
            last = final[:1]
            middle_other = swap_rep(stack([updated, near, far]))
            summed = parts[0] + wide(final[1:]) + wide(crossed)
            held = [updated, near, far, last]
            others = [(middle_other, [0, 1, 2]), (swap_rep(last), [3])]
            window, settled = [third, pair], [middle_other] if step > 0 else []
        else:
            bits = [1 << i for i in range(n_var.bit_length() - 1)]
            found = {0: updated}
            for bit in reversed(bits):
                for d in list(found):
                    found[d | bit] = shift_var(found[d], bit)
            held = [found[d] for d in range(n_var)]
            sums = dict(enumerate(parts))
            for bit in bits:
                for d in sorted(sums, reverse=True):
                    if d & bit:
                        sums[d ^ bit] = sums[d ^ bit] + wide(
                            shift_var(narrow(sums.pop(d)), bit)
                        )
            summed = sums[0]
            others = [(swap_rep(stack(held)), list(range(n_var)))]
            window, settled = [], []

        if step == 0:
            swapped, entries, _ = swap_all([sent], [sign_labels], [], window)
            jobs = jobs_of(entries)
        else:
            swapped, entries, offset = swap_all(incoming, incoming_labels, [left_own], window)
            tail = [None] * offset + [row_place(1)]
            jobs = jobs_of(entries)
            jobs.append(([(left_own, [row_place(0)]), (swapped, tail)], rows))
        found = list(unpack(meta, jobs))
        unpacked += found
        if step > 0:
            left[0].append(found.pop())
        for index in range(groups):
            right[1 + index].append(found.pop(0))
            left[1 + index].append(right[1 + index][0] if step == 0 else found.pop(0))

        left_own = narrow(wide(tie(left_own, swapped, *settled)) + inverse * summed)
        if step == 2 and n_var == 4:
            ending = stack([last, left_own])
            ending_other = swap_rep(ending)
            others = [(middle_other, [0, 1, 2]), (ending_other, [3, None])]
            incoming = [from_probes(stack(held[:3])), from_probes(ending)]
            incoming_labels = [[0, 1, 2], [3, "row"]]
        else:
            incoming = [from_probes(stack(held + [left_own]))]
            incoming_labels = [list(range(n_var)) + ["row"]]
        sources = place([(array, [d]) for d, array in enumerate(held)], 0) + place(others, 1)
        if step < 2:
            keep, send = backward(
                meta, cols, other_columns, near_blocks, other_blocks, left_own, blocks, []
            )
            received = swap_rep(send)
            panel, updated = forward(
                meta, cols, other_columns, near_blocks, other_blocks, sources, blocks, inverse,
                [send],
            )
            right[0].append(panel)

    jobs = [(sources, blocks)]
    if n_var == 4:
        rows_other = (ending_other, [None, row_place(1)])
    else:
        rows_other = (swap_rep(left_own), [row_place(1)])
    jobs.append(([(left_own, [row_place(0)]), rows_other], rows))
    ready = list(unpack(meta, jobs))
    right[0].append(ready[0])
    left[0].append(ready[1])
    entries = []
    for array, labels in zip(incoming, incoming_labels):
        tokens = ready + unpacked if array is incoming[-1] else []
        _, entry, _ = swap_all([array], [labels], [], tokens)
        entries += entry
    found = list(unpack(meta, jobs_of(entries)))
    for index in range(groups):
        right[1 + index].append(found.pop(0))
        left[1 + index].append(found.pop(0))

    lefts = [group[t] for t in range(4) for group in left]
    rights = [group[3 - t] for t in range(4) for group in right]
    scale = 1.0 / (count * n_probe)
    return gradient(meta, cols, lefts, rights, rows, slots, scale)


def solution(mesh):
    return jax.shard_map(
        local,
        mesh=mesh,
        in_specs=(
            P(("groups", "var"), "rep", None, None),
            P(("groups", "var"), "rep"),
            P("groups", "probe", None),
        ),
        out_specs=P(("groups", "var"), "rep", None, None),
        check_vma=False,
    )
```
